32 devices in a mesh: groups: 2 (over x), band: 8 (over z, y), sub: 2 (over core).
Axes of the slice: x: 2, y: 2, z: 4, core: 2. Of those that a mesh axis runs over, the one named last changes fastest.
Arguments:
- state: bfloat16 [154, 96, 240], P('groups', 'band', 'sub'), parts along dimension 0, may hold values from -6 to 6
- target: bfloat16 [154, 96, 240], P('groups', 'band', 'sub'), parts along dimension 0, may hold values from -6 to 6
- tile_plan: int32 [16, 20], P('groups'), parts along dimension 0, may hold values from -1 to 31, as said below
- w_enc: bfloat16 [77, 256], replicated, may hold values from -0.625 to 0.625
- dw_kernel: bfloat16 [49, 256], replicated, may hold values from -0.875 to 0.875
- norm_gain: float32 [256], replicated, may hold values from 0.1 to 1.9
- w_up: bfloat16 [256, 1024], replicated, may hold values from -0.375 to 0.375
- w_down: bfloat16 [1024, 256], replicated, may hold values from -0.1875 to 0.1875
- w_dec: bfloat16 [256, 77], replicated, may hold values from -0.375 to 0.375
Outputs:
- predicted_state: bfloat16 [154, 96, 240], P('groups', 'band', 'sub'), parts along dimension 0
- loss: float32 [2], P('groups'), parts along dimension 0
- grad_w_enc: float32 [154, 256], P('groups'), parts along dimension 0
- grad_dw_kernel: float32 [98, 256], P('groups'), parts along dimension 0
- grad_norm_gain: float32 [512], P('groups'), parts along dimension 0
- grad_w_up: float32 [512, 1024], P('groups'), parts along dimension 0
- grad_w_down: float32 [2048, 256], P('groups'), parts along dimension 0
- grad_w_dec: float32 [512, 77], P('groups'), parts along dimension 0
The draws below stay inside these ranges and needn't reach their ends.
There are 2 independent parts, one for each index of `groups`. The reference program is written for one: setup_inputs(seed, part) draws one part's arguments, and reference() takes and returns one part's arrays. A program takes and returns all parts, laid end to end along the dimension named above; an argument that names none is the same for every part. Nothing has to cross between parts.
Inputs may be any that keep to these rules, and one draw needn't show every extreme that they name: `tile_plan`: for a wet tile held by band index e in one half of sub, the value d * 4 + s names band index d and slot s of a computing device in the same half of sub, where d - e taken cyclically over the band indices lies between -2 and 2. In each half of sub every slot of every band index is named by exactly one wet tile. Wet tiles come in pairs of longitude neighbours (tile columns 2m and 2m+1 of one device's 10 columns) that go to one device in slots 2k and 2k+1, and one device holds at most one such pair for one computing band, so at most 2 tiles; every draw reaches that.
All inputs are finite; a program needn't handle non-finite values.
Results may differ from the reference program's by a relative error of at most 0.0042.
Values may be sent and summed in bfloat16 or wider, within the bound.
No kernel may reach another device: no remote copies, remote signals or barrier semaphores. Data moves between devices by JAX's collectives and lax.ppermute only.
A program may use at most 64 MiB of HBM per device.

```python
import math
import jax
import jax.numpy as jnp
import numpy as np
from jax import lax

C = 77
W = 256
HID = 1024
KSIZE = 7
PATCH_WIDTH = 12
TR = 1
TC = 10
TILES_CMP = 4
REACH = 2
ROWS_T = 8
ROWS = 96
COLS = 240
N_BAND = 8
N_SUB = 2


def column_plan(key):
    band_total = ROWS_T // TR
    pair_count = TR * TC // 2
    reach_span = 2 * REACH + 1
    half_slots = TILES_CMP // 2
    key_offset, key_position = jax.random.split(key, 2)
    offset_score = jax.random.randint(key_offset, (band_total, reach_span), 0, 1024) * reach_span
    offset_score = offset_score + jnp.arange(reach_span, dtype=jnp.int32)[None, :]
    chosen = jnp.argsort(offset_score, axis=1)[:, :half_slots].astype(jnp.int32)
    position_score = jax.random.randint(key_position, (band_total, pair_count), 0, 1024) * pair_count
    position_score = position_score + jnp.arange(pair_count, dtype=jnp.int32)[None, :]
    position_of = jnp.argsort(position_score, axis=1)[:, :reach_span].astype(jnp.int32)
    dest_band = jnp.arange(band_total, dtype=jnp.int32)[:, None]
    source_band = (dest_band - (chosen - REACH)) % band_total
    position = position_of[source_band, chosen]
    first_value = dest_band * TILES_CMP + 2 * jnp.arange(half_slots, dtype=jnp.int32)[None, :]
    first_tile = jnp.full((band_total, pair_count), -1, jnp.int32).at[source_band, position].set(first_value)
    second_tile = jnp.where(first_tile >= 0, first_tile + 1, -1)
    first_tile = first_tile.reshape(band_total, TR, TC // 2)
    second_tile = second_tile.reshape(band_total, TR, TC // 2)
    tile_values = jnp.stack([first_tile, second_tile], axis=-1).reshape(band_total * TR, TC)
    return tile_values.astype(jnp.int32)


def draw_tile_plan(key, part):
    west_half = column_plan(jax.random.fold_in(key, 11))
    east_half = column_plan(jax.random.fold_in(key, 12))
    return jnp.concatenate([west_half, east_half], axis=1)


def steps_of(rng, extent, shards, smallest, high):
    def one(dim, parts):
        heights = jax.random.uniform(jax.random.fold_in(jax.random.fold_in(rng, 6), dim), (parts,), jnp.float32, smallest / len(shards), high / len(shards))
        return jnp.repeat(jnp.exp(heights), extent[dim] // parts).reshape((-1,) + (1,) * (len(extent) - dim - 1))

    factor_of = one(*shards[0])
    for cut in shards[1:]:
        factor_of = factor_of * one(*cut)
    return factor_of


def normal_values(key, shape, scale, limit, cuts=(), held_as=jnp.bfloat16):
    array = scale * jax.random.normal(key, shape, jnp.float32)
    if cuts:
        array = array * steps_of(key, shape, cuts, -0.22, 0.18)
    return jnp.clip(array, -limit, limit).astype(held_as)


def setup_inputs(seed: int = 0, part: int = 0) -> dict:
    keys = jax.random.split(jax.random.key(seed), 10)
    own_keys = jax.random.split(jax.random.fold_in(keys[9], part), 10)
    state = normal_values(own_keys[0], (C, ROWS, COLS), 1.0, 6.0, ((1, 8), (2, 2)))
    target = normal_values(own_keys[1], (C, ROWS, COLS), 1.0, 6.0, ((1, 8), (2, 2)))
    tile_plan = draw_tile_plan(jax.random.fold_in(jax.random.fold_in(keys[9], part), 71), part)
    w_enc = normal_values(keys[3], (C, W), C ** -0.5, 0.625)
    dw_kernel = normal_values(keys[4], (KSIZE * KSIZE, W), (KSIZE * KSIZE) ** -0.5, 0.875)
    norm_gain = jnp.clip(1.0 + 0.18 * jax.random.normal(keys[5], (W,), jnp.float32), 0.1, 1.9)
    w_up = normal_values(keys[6], (W, HID), W ** -0.5, 0.375)
    w_down = normal_values(keys[7], (HID, W), HID ** -0.5, 0.1875)
    w_dec = normal_values(keys[8], (W, C), W ** -0.5, 0.375)
    return {"state": state, "target": target, "tile_plan": tile_plan, "w_enc": w_enc, "dw_kernel": dw_kernel, "norm_gain": norm_gain, "w_up": w_up, "w_down": w_down, "w_dec": w_dec}


def contract(form, left, right):
    return jnp.einsum(form, left.astype(jnp.float32), right.astype(jnp.float32))

def tile_terms(tiles_in, desired_patches, ocean_indicator, reciprocal_cells, w_enc, dw_kernel, norm_gain, w_up, w_down, w_dec):
    patch_identifier = tiles_in.shape[0]
    feature_depth = tiles_in.shape[1]
    hidden_width = w_enc.shape[1]
    tile_edge = PATCH_WIDTH + KSIZE - 1
    rim_cells = KSIZE // 2
    encoded = contract('bcp,cw->bpw', tiles_in, w_enc).astype(jnp.bfloat16)
    encoded = encoded.reshape(patch_identifier, tile_edge, tile_edge, hidden_width)
    kernel = dw_kernel.astype(jnp.float32)
    mixed_conv = jnp.zeros((patch_identifier, PATCH_WIDTH, PATCH_WIDTH, hidden_width), jnp.float32)
    for offset in range(KSIZE * KSIZE):
        row_shift, col_shift = divmod(offset, KSIZE)
        window = encoded[:, row_shift:row_shift + PATCH_WIDTH, col_shift:col_shift + PATCH_WIDTH, :].astype(jnp.float32)
        mixed_conv = mixed_conv + window * kernel[offset]
    centre_mean = lax.optimization_barrier(jnp.mean(mixed_conv, axis=-1, keepdims=True))
    centred = mixed_conv - centre_mean
    variance = lax.optimization_barrier(jnp.mean(centred * centred, axis=-1, keepdims=True))
    inv_std = lax.rsqrt(variance + 1e-06)
    normed = centred * inv_std
    gain_vec = norm_gain.astype(jnp.float32)
    scaled = (normed * gain_vec).astype(jnp.bfloat16).reshape(-1, hidden_width)
    pre_act = jnp.dot(scaled, w_up, preferred_element_type=jnp.float32)
    activated = jax.nn.gelu(pre_act).astype(jnp.bfloat16)
    expanded = jnp.dot(activated, w_down, preferred_element_type=jnp.float32)
    centre = encoded[:, rim_cells:rim_cells + PATCH_WIDTH, rim_cells:rim_cells + PATCH_WIDTH, :].reshape(-1, hidden_width)
    residual = (centre.astype(jnp.float32) + expanded).astype(jnp.bfloat16)
    readout_result = jnp.dot(residual, w_dec, preferred_element_type=jnp.float32)
    readout_result = readout_result.reshape(patch_identifier, PATCH_WIDTH * PATCH_WIDTH, feature_depth).transpose(0, 2, 1)
    unchanged_baseline = tiles_in.reshape(patch_identifier, feature_depth, tile_edge, tile_edge)
    unchanged_baseline = unchanged_baseline[:, :, rim_cells:rim_cells + PATCH_WIDTH, rim_cells:rim_cells + PATCH_WIDTH]
    predicted_state = unchanged_baseline.reshape(patch_identifier, feature_depth, PATCH_WIDTH * PATCH_WIDTH).astype(jnp.float32) + readout_result
    prediction_misfit = (predicted_state - desired_patches.astype(jnp.float32)) * ocean_indicator[:, None, None]
    objective_sum = jnp.sum(prediction_misfit * prediction_misfit) * reciprocal_cells
    upstream_sensitivity = (prediction_misfit * (2.0 * reciprocal_cells)).transpose(0, 2, 1).reshape(-1, feature_depth).astype(jnp.bfloat16)
    readout_sensitivity = jnp.dot(residual.T, upstream_sensitivity, preferred_element_type=jnp.float32)
    grad_res = jnp.dot(upstream_sensitivity, w_dec.T, preferred_element_type=jnp.float32).astype(jnp.bfloat16)
    contracting_sensitivity = jnp.dot(activated.T, grad_res, preferred_element_type=jnp.float32)
    grad_act = jnp.dot(grad_res, w_down.T, preferred_element_type=jnp.float32)
    grad_pre = jax.vjp(jax.nn.gelu, pre_act)[1](grad_act)[0].astype(jnp.bfloat16)
    widening_sensitivity = jnp.dot(scaled.T, grad_pre, preferred_element_type=jnp.float32)
    grad_scaled = jnp.dot(grad_pre, w_up.T, preferred_element_type=jnp.float32)
    grad_scaled = grad_scaled.reshape(patch_identifier, PATCH_WIDTH, PATCH_WIDTH, hidden_width)
    norm_scale_sensitivity = lax.optimization_barrier(jnp.sum(grad_scaled * normed, axis=(0, 1, 2)))
    grad_normed = grad_scaled * gain_vec
    grad_conv = inv_std * (grad_normed - lax.optimization_barrier(jnp.mean(grad_normed, axis=-1, keepdims=True)) - normed * lax.optimization_barrier(jnp.mean(grad_normed * normed, axis=-1, keepdims=True)))
    grad_enc = jnp.zeros((patch_identifier, tile_edge, tile_edge, hidden_width), jnp.float32)
    grad_enc = grad_enc.at[:, rim_cells:rim_cells + PATCH_WIDTH, rim_cells:rim_cells + PATCH_WIDTH, :].add(grad_res.astype(jnp.float32).reshape(patch_identifier, PATCH_WIDTH, PATCH_WIDTH, hidden_width))
    kernel_rows = []
    for offset in range(KSIZE * KSIZE):
        row_shift, col_shift = divmod(offset, KSIZE)
        window = encoded[:, row_shift:row_shift + PATCH_WIDTH, col_shift:col_shift + PATCH_WIDTH, :].astype(jnp.float32)
        kernel_rows.append(lax.optimization_barrier(jnp.sum(grad_conv * window, axis=(0, 1, 2))))
        grad_enc = grad_enc.at[:, row_shift:row_shift + PATCH_WIDTH, col_shift:col_shift + PATCH_WIDTH, :].add(grad_conv * kernel[offset])
    stencil_sensitivity = jnp.stack(kernel_rows)
    grad_enc_b = grad_enc.astype(jnp.bfloat16).reshape(patch_identifier, tile_edge * tile_edge, hidden_width)
    entry_sensitivity = contract('bcp,bpw->cw', tiles_in, grad_enc_b)
    return (predicted_state, objective_sum, (entry_sensitivity, stencil_sensitivity, norm_scale_sensitivity, widening_sensitivity, contracting_sensitivity, readout_sensitivity))

def run_blocks(tiles_in, desired_patches, ocean_indicator, reciprocal_cells, weights):
    patch_identifier = tiles_in.shape[0]
    block_size = math.gcd(patch_identifier, 2)
    block_count = patch_identifier // block_size
    empty_grads = tuple((jnp.zeros(weight.shape, jnp.float32) for weight in weights))

    def one_block(running, pieces):
        predicted, objective_sum, gradients = tile_terms(pieces[0], pieces[1], pieces[2], reciprocal_cells, *weights)
        summed = tuple((first + second for first, second in zip(running[1], gradients)))
        return ((running[0] + objective_sum, summed), predicted)
    start = (jnp.zeros((), jnp.float32), empty_grads)
    pieces = (tiles_in.reshape((block_count, block_size) + tiles_in.shape[1:]), desired_patches.reshape((block_count, block_size) + desired_patches.shape[1:]), ocean_indicator.reshape(block_count, block_size))
    (objective_sum, gradients), predicted = lax.scan(one_block, start, pieces)
    return (predicted.reshape((patch_identifier,) + predicted.shape[2:]), objective_sum, gradients)

def reference(state, target, tile_plan, w_enc, dw_kernel, norm_gain, w_up, w_down, w_dec):
    feature_depth = state.shape[0]
    rim_cells = KSIZE // 2
    tile_edge = PATCH_WIDTH + KSIZE - 1
    tile_rows = state.shape[1] // PATCH_WIDTH
    tile_cols = state.shape[2] // PATCH_WIDTH
    total_tiles = tile_rows * tile_cols
    wet_total = N_BAND * N_SUB * TILES_CMP
    lon_wide = jnp.concatenate([state[:, :, -rim_cells:], state, state[:, :, :rim_cells]], axis=2)
    padded = jnp.pad(lon_wide, ((0, 0), (rim_cells, rim_cells), (0, 0)))
    row_index = np.arange(tile_rows)[:, None] * PATCH_WIDTH + np.arange(tile_edge)[None, :]
    col_index = np.arange(tile_cols)[:, None] * PATCH_WIDTH + np.arange(tile_edge)[None, :]
    picked = padded[:, row_index, :][:, :, :, col_index]
    tiles_in = picked.transpose(1, 3, 0, 2, 4).reshape(total_tiles, feature_depth, tile_edge * tile_edge)
    desired_patches = target.reshape(feature_depth, tile_rows, PATCH_WIDTH, tile_cols, PATCH_WIDTH).transpose(1, 3, 0, 2, 4)
    desired_patches = desired_patches.reshape(total_tiles, feature_depth, PATCH_WIDTH * PATCH_WIDTH)
    wet_tiles = tile_plan >= 0
    reciprocal_cells = 1.0 / (jnp.sum(wet_tiles.astype(jnp.float32)) * (feature_depth * PATCH_WIDTH * PATCH_WIDTH))
    flat_wet = wet_tiles.reshape(-1)
    order_key = jnp.where(flat_wet, 0, total_tiles).astype(jnp.int32) + jnp.arange(total_tiles, dtype=jnp.int32)
    chosen = jnp.argsort(order_key)[:wet_total].astype(jnp.int32)
    weights = (w_enc, dw_kernel, norm_gain, w_up, w_down, w_dec)
    predicted, objective_sum, gradients = run_blocks(tiles_in[chosen], desired_patches[chosen], flat_wet[chosen].astype(jnp.float32), reciprocal_cells, weights)
    placed = jnp.zeros((total_tiles, feature_depth, PATCH_WIDTH * PATCH_WIDTH), jnp.float32).at[chosen].set(predicted)
    tiles_out = placed.astype(jnp.bfloat16).reshape(tile_rows, tile_cols, feature_depth, PATCH_WIDTH, PATCH_WIDTH)
    tiles_out = tiles_out.transpose(2, 0, 3, 1, 4).reshape(feature_depth, tile_rows * PATCH_WIDTH, tile_cols * PATCH_WIDTH)
    wet_cells = jnp.repeat(jnp.repeat(wet_tiles, PATCH_WIDTH, axis=0), PATCH_WIDTH, axis=1)
    new_field = jnp.where(wet_cells[None], tiles_out, state)
    return (new_field, objective_sum.reshape(1), gradients[0], gradients[1], gradients[2], gradients[3], gradients[4], gradients[5])
```

```python
import math

import jax
import jax.numpy as jnp
from jax import lax
from jax.experimental import pallas as pl
from jax.experimental.pallas import tpu as pltpu
from jax.sharding import PartitionSpec as P

F32 = jnp.float32
BF16 = jnp.bfloat16

KSIZE = 7
RIM = KSIZE // 2
PATCH = 12
LANES = 128
SUBL = 8
SMALL_ROWS = 256
AT_DEC = 80
AT_DW = 160
AT_GAIN = 216
AT_LOSS = 224
GELU_A = math.sqrt(2.0 / math.pi)
GELU_B = GELU_A * 0.044715


def nn(a, b):
    return lax.dot_general(a, b, (((1,), (0,)), ((), ())), preferred_element_type=F32)


def nt(a, b):
    return lax.dot_general(a, b, (((1,), (1,)), ((), ())), preferred_element_type=F32)


def tn(a, b):
    return lax.dot_general(a, b, (((0,), (0,)), ((), ())), preferred_element_type=F32)


def strip_column(shape, strip, shift):
    r = lax.broadcasted_iota(jnp.int32, shape, 0)
    return (r & (SUBL - 1)) * strip + (r >> 3) - shift


def step_kernel(
    plan_ref, st_ref, top_ref, bot_ref, e_ref, tgt_ref,
    wenc_ref, dw_ref, gain_ref, wup_ref, wdown_ref, wdec_ref,
    new_ref, keep_ref, send_ref,
    enc_ref, xa_ref, kb_ref, nrm_ref, istd_ref, gr_ref, act_ref, dg_ref, gp_ref, gs_ref, sc_ref,
    rs_ref, ge_ref, acc_ref, small_ref,
):
    rows, chans, cols = st_ref.shape
    width = wenc_ref.shape[1]
    hid = wup_ref.shape[1]
    strip = cols // SUBL
    wide = strip + 2 * RIM
    main = strip * SUBL
    wmain = wide * SUBL
    band = lax.axis_index("band")
    sub = lax.axis_index("sub")
    tiles = cols // PATCH

    col_w = strip_column((wmain, cols), strip, RIM)
    pick = (col_w == lax.broadcasted_iota(jnp.int32, (wmain, cols), 1)).astype(BF16)
    edge = lax.broadcasted_iota(jnp.int32, (wmain, 2 * RIM), 1)
    edge_col = jnp.where(edge < RIM, edge - RIM, edge - RIM + cols)
    pick_edge = (strip_column((wmain, 2 * RIM), strip, RIM) == edge_col).astype(BF16)
    full = lax.broadcasted_iota(jnp.int32, (wmain, cols + 2 * RIM), 1)
    left = full - cols - RIM
    full_col = jnp.where(full < cols, full, jnp.where(left < 0, left, left + cols))
    pick_full = (strip_column(full.shape, strip, RIM) == full_col).astype(BF16)
    col_c = strip_column((main, cols), strip, 0)
    place = (col_c == lax.broadcasted_iota(jnp.int32, (main, cols), 1)).astype(BF16)

    wet_all = (plan_ref[...] >= 0).astype(F32)
    inv = 1.0 / (jnp.sum(wet_all, axis=(0, 1), keepdims=True) * float(chans * rows * PATCH))
    wet_row = (plan_ref[pl.ds(band, 1), :] >= 0).astype(F32)
    n_cols = wet_row.shape[1]
    at = lax.broadcasted_iota(jnp.int32, (main, n_cols), 1) - sub * tiles
    cc = strip_column((main, n_cols), strip, 0)
    in_tile = (cc >= at * PATCH) & (cc < at * PATCH + PATCH)
    wet_rows = jnp.sum(jnp.where(in_tile, wet_row, 0.0), axis=1, keepdims=True)
    at_x = lax.broadcasted_iota(jnp.int32, (n_cols, cols), 0) - sub * tiles
    x_x = lax.broadcasted_iota(jnp.int32, (n_cols, cols), 1)
    in_x = ((x_x >= at_x * PATCH) & (x_x < at_x * PATCH + PATCH)).astype(BF16)
    wet_x = nn(jnp.broadcast_to(wet_row, (SUBL, n_cols)).astype(BF16), in_x)[0:1]

    for o in range(KSIZE * KSIZE):
        kb_ref[o] = jnp.broadcast_to(dw_ref[o : o + 1, :].astype(F32), (SUBL, width))

    def encode(y, xa):
        xa_ref[y] = xa
        enc_ref[y] = nn(xa.astype(BF16), wenc_ref[...]).astype(BF16).astype(F32)

    def enc_top(i, c):
        encode(i, nt(pick_full, top_ref[i]))
        return c

    def enc_mid(i, c):
        encode(i + RIM, nt(pick, st_ref[i]) + nt(pick_edge, e_ref[i]))
        return c

    def enc_bot(i, c):
        encode(i + RIM + rows, nt(pick_full, bot_ref[i]))
        return c

    lax.fori_loop(0, RIM, enc_top, 0)
    lax.fori_loop(0, rows, enc_mid, 0)
    lax.fori_loop(0, RIM, enc_bot, 0)

    def conv(y, c):
        for h in range(width // LANES):
            ln = slice(h * LANES, (h + 1) * LANES)
            acc = jnp.zeros((strip, SUBL, LANES), F32)
            for a in range(KSIZE):
                e = enc_ref[y + a, :, ln].reshape(wide, SUBL, LANES)
                for b in range(KSIZE):
                    acc = acc + e[b : b + strip] * kb_ref[a * KSIZE + b, :, ln]
            nrm_ref[y, :, ln] = acc.reshape(main, LANES)
        v = nrm_ref[y]
        cen = v - jnp.mean(v, axis=-1, keepdims=True)
        istd = lax.rsqrt(jnp.mean(cen * cen, axis=-1, keepdims=True) + 1e-06)
        nrm_ref[y] = cen * istd
        istd_ref[y] = jnp.broadcast_to(istd, (main, LANES))
        return c

    lax.fori_loop(0, rows, conv, 0)

    small_ref[...] = jnp.zeros_like(small_ref)
    acc_ref[...] = jnp.zeros_like(acc_ref)
    ge_ref[...] = jnp.zeros_like(ge_ref)
    gain = gain_ref[...]
    group = 4
    chunk = group * main
    blocks = hid // width
    wetg = jnp.concatenate([wet_rows] * group, axis=0)

    def mlp(k, loss):
        y0 = k * group
        r0 = pl.multiple_of(k * chunk, chunk)
        nrm = nrm_ref[pl.ds(y0, group)].reshape(chunk, width)
        scaled = (nrm * gain).astype(BF16)
        sc_ref[pl.ds(r0, chunk), :] = scaled
        centre = enc_ref[pl.ds(y0 + RIM, group), RIM * SUBL : RIM * SUBL + main, :]
        rs_ref[...] = centre.reshape(chunk, width)

        def up(n, c):
            n0 = pl.multiple_of(n * width, width)
            v = nn(sc_ref[pl.ds(r0, chunk), :], wup_ref[:, pl.ds(n0, width)])
            vv = v * v
            t = jnp.tanh(v * (GELU_A + GELU_B * vv))
            hv = 0.5 * v
            act = (hv + hv * t).astype(BF16)
            dg_ref[:, pl.ds(n0, width)] = 0.5 + 0.5 * t + hv * (1.0 - t * t) * (
                GELU_A + 3.0 * GELU_B * vv
            )
            act_ref[pl.ds(r0, chunk), pl.ds(n0, width)] = act
            rs_ref[...] += nn(act, wdown_ref[pl.ds(n0, width), :])
            return c

        lax.fori_loop(0, blocks, up, 0)
        residual = rs_ref[...].astype(BF16)
        base = xa_ref[pl.ds(y0 + RIM, group), RIM * SUBL : RIM * SUBL + main, :]
        pred = base.reshape(chunk, chans) + nn(residual, wdec_ref[...])
        goal = jnp.concatenate([nt(place, tgt_ref[y0 + i]) for i in range(group)], axis=0)
        mis = (pred - goal) * wetg
        for i in range(group):
            back = tn(pred[i * main : (i + 1) * main].astype(BF16), place)
            new_ref[y0 + i] = jnp.where(wet_x > 0.5, back.astype(BF16), st_ref[y0 + i])
        loss = loss + jnp.sum(mis * mis, axis=(0, 1), keepdims=True)
        gout = (mis * (2.0 * inv)).astype(BF16)
        small_ref[AT_DEC : AT_DEC + chans, :] += tn(gout, residual)
        gres = nt(gout, wdec_ref[...]).astype(BF16)
        gr_ref[pl.ds(r0, chunk), :] = gres
        for i in range(group):
            ge_ref[y0 + RIM + i, RIM * SUBL : RIM * SUBL + main, :] = gres[
                i * main : (i + 1) * main
            ].astype(F32)
        gs_ref[...] = jnp.zeros_like(gs_ref)

        def down(n, c):
            n0 = pl.multiple_of(n * width, width)
            ga = nt(gr_ref[pl.ds(r0, chunk), :], wdown_ref[pl.ds(n0, width), :])
            gp = (ga * dg_ref[:, pl.ds(n0, width)]).astype(BF16)
            gp_ref[pl.ds(r0, chunk), pl.ds(n0, width)] = gp
            gs_ref[...] += nt(gp, wup_ref[:, pl.ds(n0, width)])
            return c

        lax.fori_loop(0, blocks, down, 0)
        gs = gs_ref[...]
        nrm = nrm_ref[pl.ds(y0, group)].reshape(chunk, width)
        prod = gs * nrm
        small_ref[AT_GAIN : AT_GAIN + 1, :] += jnp.sum(prod, axis=0, keepdims=True)
        g = gs * gain
        m1 = jnp.mean(g, axis=-1, keepdims=True)
        m2 = jnp.mean(g * nrm, axis=-1, keepdims=True)
        gc = g - m1 - nrm * m2
        istd = istd_ref[pl.ds(y0, group)].reshape(chunk, LANES)
        for h in range(width // LANES):
            ln = slice(h * LANES, (h + 1) * LANES)
            nrm_ref[pl.ds(y0, group), :, ln] = (gc[:, ln] * istd).reshape(group, main, LANES)
        return loss

    loss = lax.fori_loop(0, rows // group, mlp, jnp.zeros((1, 1), F32))
    lane = lax.broadcasted_iota(jnp.int32, (1, width), 1)
    rest = jnp.where(lane == band * lax.axis_size("sub") + sub, loss * inv, 0.0)
    for i in range(3):
        term = rest.astype(BF16).astype(F32)
        small_ref[AT_LOSS + i : AT_LOSS + i + 1, :] = term
        rest = rest - term

    n_piece = keep_ref.shape[0]
    tall = width // n_piece

    def wgrad(n, c):
        n0 = pl.multiple_of(n * width, width)
        g_up = tn(sc_ref[...], gp_ref[:, pl.ds(n0, width)])
        g_down = tn(gr_ref[...], act_ref[:, pl.ds(n0, width)])
        first = sub == 0
        keep = jnp.where(first, g_up, g_down).reshape(n_piece, tall, width)
        send = jnp.where(first, g_down, g_up).reshape(n_piece, tall, width)
        keep_ref[:, 0:tall, pl.ds(n0, width)] = keep
        send_ref[:, 0:tall, pl.ds(n0, width)] = send.astype(BF16)
        return c

    lax.fori_loop(0, blocks, wgrad, 0)

    def conv_back(y, c):
        for h in range(width // LANES):
            ln = slice(h * LANES, (h + 1) * LANES)
            g = nrm_ref[y, :, ln].reshape(strip, SUBL, LANES)
            for a in range(KSIZE):
                e = enc_ref[y + a, :, ln].reshape(wide, SUBL, LANES)
                out = [ge_ref[y + a, j * SUBL : (j + 1) * SUBL, ln] for j in range(wide)]
                for b in range(KSIZE):
                    o = a * KSIZE + b
                    acc_ref[o, :, ln] += jnp.sum(g * e[b : b + strip], axis=0)
                    k = kb_ref[o, :, ln]
                    for j in range(strip):
                        out[j + b] = out[j + b] + g[j] * k
                for j in range(wide):
                    ge_ref[y + a, j * SUBL : (j + 1) * SUBL, ln] = out[j]
        return c

    lax.fori_loop(0, rows, conv_back, 0)
    high = rows + 2 * RIM
    xa = xa_ref[...].reshape(high * wmain, chans).astype(BF16)
    ge = ge_ref[...].reshape(high * wmain, width).astype(BF16)
    small_ref[0:chans, :] = tn(xa, ge)
    small_ref[AT_DW : AT_DW + KSIZE * KSIZE, :] = jnp.sum(acc_ref[...], axis=1)

    half = SMALL_ROWS // 2
    part = half // n_piece
    flat = part // blocks
    keep = small_ref[pl.ds(pl.multiple_of(sub * half, half), half), :]
    send = small_ref[pl.ds(pl.multiple_of((1 - sub) * half, half), half), :]
    keep = keep.reshape(n_piece, part, width)
    send = send.reshape(n_piece, part, width)
    for q in range(blocks):
        ln = slice(q * width, (q + 1) * width)
        keep_ref[:, tall : tall + flat, ln] = keep[:, q * flat : (q + 1) * flat]
        send_ref[:, tall : tall + flat, ln] = send[:, q * flat : (q + 1) * flat].astype(BF16)


def vmem(n):
    return [pl.BlockSpec(memory_space=pltpu.VMEM) for _ in range(n)]


def swapped(value, axis, d):
    size = lax.axis_size(axis)
    return lax.ppermute(value, axis, [(i, i ^ d) for i in range(size)])


def pick_kernel(n, keep_ref, recv_ref, own_ref, *out_refs):
    band = lax.axis_index("band")
    own_ref[...] = keep_ref[band] + recv_ref[band].astype(F32)
    for d in range(1, n):
        out_refs[d - 1][...] = (keep_ref[band ^ d] + recv_ref[band ^ d].astype(F32)).astype(BF16)


def add_kernel(n, own_ref, *refs):
    total = own_ref[...]
    for d in range(1, n):
        total = total + refs[d - 1][...].astype(F32)
    refs[n - 1][...] = total.astype(BF16)


def join_kernel(n, *refs):
    band = lax.axis_index("band")
    for d in range(n):
        refs[n][band ^ d] = refs[d][...]


def spread_kernel(mine_ref, other_ref, up_ref, down_ref, enc_ref, dw_ref, gain_ref, dec_ref, loss_ref, small_ref):
    n, deep, hid = mine_ref.shape
    width = up_ref.shape[0]
    blocks = hid // width
    tall = width // n
    flat = deep - tall
    half = SMALL_ROWS // 2
    sub = lax.axis_index("sub")

    def put(up_from, down_from, first):
        up_ref[...] = up_from[:, 0:tall, :].astype(F32).reshape(width, hid)
        for q in range(blocks):
            ln = slice(q * width, (q + 1) * width)
            down_ref[ln, :] = down_from[:, 0:tall, ln].astype(F32).reshape(width, width).T
            for i, ref in enumerate((up_from, down_from)):
                for p in range(n):
                    r = i * half + p * flat * blocks + q * flat
                    small_ref[r : r + flat, :] = ref[p, tall:deep, ln].astype(F32)

    @pl.when(sub == 0)
    def _():
        put(mine_ref, other_ref, 0)

    @pl.when(sub != 0)
    def _():
        put(other_ref, mine_ref, 1)

    chans = enc_ref.shape[0]
    enc_ref[...] = small_ref[0:chans, :]
    dec_ref[...] = small_ref[AT_DEC : AT_DEC + AT_DW - AT_DEC, :].T[:, 0:chans]
    dw_ref[...] = small_ref[AT_DW : AT_DW + KSIZE * KSIZE, :]
    gain_ref[...] = small_ref[AT_GAIN : AT_GAIN + 1, :]
    loss_ref[...] = jnp.sum(small_ref[AT_LOSS : AT_LOSS + 3, :], axis=(0, 1), keepdims=True)


def summed(keep, send, shapes):
    n, deep, hid = keep.shape
    recv = swapped(send, "sub", 1)
    piece = (deep, hid)
    outs = [jax.ShapeDtypeStruct(piece, F32)] + [jax.ShapeDtypeStruct(piece, BF16)] * (n - 1)
    parts = pl.pallas_call(
        lambda *r: pick_kernel(n, *r),
        out_shape=outs, in_specs=vmem(2), out_specs=vmem(n), name="pick",
    )(keep, recv)
    got = [swapped(parts[d], "band", d) for d in range(1, n)]
    total = pl.pallas_call(
        lambda *r: add_kernel(n, *r),
        out_shape=jax.ShapeDtypeStruct(piece, BF16),
        in_specs=vmem(n), out_specs=vmem(1)[0], name="add",
    )(parts[0], *got)
    every = [total] + [swapped(total, "band", d) for d in range(1, n)]
    half = pl.pallas_call(
        lambda *r: join_kernel(n, *r),
        out_shape=jax.ShapeDtypeStruct((n,) + piece, BF16),
        in_specs=vmem(n), out_specs=vmem(1)[0], name="join",
    )(*every)
    other = swapped(half, "sub", 1)
    return pl.pallas_call(
        spread_kernel,
        out_shape=[jax.ShapeDtypeStruct(s, F32) for s in shapes],
        in_specs=vmem(2), out_specs=vmem(len(shapes)),
        scratch_shapes=[pltpu.VMEM((SMALL_ROWS, shapes[0][0]), F32)],
        name="spread",
    )(half, other)


def shards(state, target, tile_plan, w_enc, dw_kernel, norm_gain, w_up, w_down, w_dec):
    chans, rows, cols = state.shape
    width = w_enc.shape[1]
    hid = w_up.shape[1]
    main = cols
    wmain = cols + 2 * RIM * SUBL
    high = rows + 2 * RIM
    n_band = lax.axis_size("band")

    st = state.transpose(1, 0, 2)
    tgt = target.transpose(1, 0, 2)
    edges = jnp.concatenate([st[:, :, cols - RIM :], st[:, :, :RIM]], axis=2)
    other = swapped(edges, "sub", 1)
    up = [(i, i + 1) for i in range(n_band - 1)]
    down = [(j, i) for i, j in up]
    last = jnp.concatenate([st[rows - RIM :], other[rows - RIM :]], axis=2)
    first = jnp.concatenate([st[:RIM], other[:RIM]], axis=2)
    top = lax.ppermute(last, "band", up)
    bot = lax.ppermute(first, "band", down)

    cells = rows * main
    chunk = 4 * main
    n = n_band
    deep = width // n + SMALL_ROWS // 2 * width // (n * hid)
    new, keep, send = pl.pallas_call(
        step_kernel,
        out_shape=[
            jax.ShapeDtypeStruct((rows, chans, cols), BF16),
            jax.ShapeDtypeStruct((n, deep, hid), F32),
            jax.ShapeDtypeStruct((n, deep, hid), BF16),
        ],
        in_specs=vmem(12), out_specs=vmem(3),
        scratch_shapes=[
            pltpu.VMEM((high, wmain, width), F32),
            pltpu.VMEM((high, wmain, chans), F32),
            pltpu.VMEM((KSIZE * KSIZE, SUBL, width), F32),
            pltpu.VMEM((rows, main, width), F32),
            pltpu.VMEM((rows, main, LANES), F32),
            pltpu.VMEM((cells, width), BF16),
            pltpu.VMEM((cells, hid), BF16),
            pltpu.VMEM((chunk, hid), F32),
            pltpu.VMEM((cells, hid), BF16),
            pltpu.VMEM((chunk, width), F32),
            pltpu.VMEM((cells, width), BF16),
            pltpu.VMEM((chunk, width), F32),
            pltpu.VMEM((high, wmain, width), F32),
            pltpu.VMEM((KSIZE * KSIZE, SUBL, width), F32),
            pltpu.VMEM((SMALL_ROWS, width), F32),
        ],
        name="step",
    )(
        tile_plan, st, top, bot, other, tgt,
        w_enc, dw_kernel, norm_gain.reshape(1, width), w_up, w_down, w_dec,
    )
    g_up, g_down, g_enc, g_dw, g_gain, g_dec, loss = summed(
        keep, send,
        [(width, hid), (hid, width), (chans, width), dw_kernel.shape, (1, width), (width, chans), (1, 1)],
    )
    return (
        new.transpose(1, 0, 2), loss.reshape(1), g_enc, g_dw, g_gain.reshape(width),
        g_up, g_down, g_dec,
    )


def solution(mesh):
    return jax.shard_map(
        shards,
        mesh=mesh,
        in_specs=(
            P("groups", "band", "sub"),
            P("groups", "band", "sub"),
            P("groups", None),
            P(),
            P(),
            P(),
            P(),
            P(),
            P(),
        ),
        out_specs=(
            P("groups", "band", "sub"),
            P("groups"),
            P("groups", None),
            P("groups", None),
            P("groups"),
            P("groups", None),
            P("groups", None),
            P("groups", None),
        ),
        check_vma=False,
    )
```

```python
import math

import jax
import jax.numpy as jnp
from jax import lax
from jax.experimental import pallas as pl
from jax.experimental.pallas import tpu as pltpu
from jax.sharding import PartitionSpec as P

F32 = jnp.float32
BF16 = jnp.bfloat16

KSIZE = 7
RIM = KSIZE // 2
PATCH = 12
LANES = 128
SUBL = 8
SMALL_ROWS = 512
GROUP = 12
UNROLL = 4
AT_DEC = 80
AT_DW = 160
AT_GAIN = 216
AT_LOSS = 224
GELU_A = math.sqrt(2.0 / math.pi)
GELU_B = GELU_A * 0.044715


def nn(a, b):
    return lax.dot_general(a, b, (((1,), (0,)), ((), ())), preferred_element_type=F32)


def nt(a, b):
    return lax.dot_general(a, b, (((1,), (1,)), ((), ())), preferred_element_type=F32)


def tn(a, b):
    return lax.dot_general(a, b, (((0,), (0,)), ((), ())), preferred_element_type=F32)


def strip_column(shape, strip, shift):
    r = lax.broadcasted_iota(jnp.int32, shape, 0)
    return (r & (SUBL - 1)) * strip + (r >> 3) - shift


def step_kernel(
    plan_ref, st_ref, near_ref, far_ref, e_ref, tgt_ref,
    wenc_ref, dw_ref, gain_ref, wup_ref, wdown_ref, wdec_ref,
    new_ref, keep_ref, send_ref,
    enc_ref, xa_ref, kb_ref, nrm_ref, istd_ref, gr_ref, act_ref, dg_ref, gp_ref, gs_ref, sc_ref,
    rs_ref, ge_ref, acc_ref, small_ref,
):
    rows, chans, cols = st_ref.shape
    width = wenc_ref.shape[1]
    hid = wup_ref.shape[1]
    strip = cols // SUBL
    wide = strip + 2 * RIM
    main = strip * SUBL
    wmain = wide * SUBL
    band = lax.axis_index("band")
    sub = lax.axis_index("sub")
    tiles = cols // PATCH

    col_w = strip_column((wmain, cols), strip, RIM)
    pick = (col_w == lax.broadcasted_iota(jnp.int32, (wmain, cols), 1)).astype(BF16)
    edge = lax.broadcasted_iota(jnp.int32, (wmain, 2 * RIM), 1)
    edge_col = jnp.where(edge < RIM, edge - RIM, edge - RIM + cols)
    pick_edge = (strip_column((wmain, 2 * RIM), strip, RIM) == edge_col).astype(BF16)
    full = lax.broadcasted_iota(jnp.int32, (wmain, cols + 2 * RIM), 1)
    left = full - cols - RIM
    full_col = jnp.where(full < cols, full, jnp.where(left < 0, left, left + cols))
    pick_full = (strip_column(full.shape, strip, RIM) == full_col).astype(BF16)
    col_c = strip_column((main, cols), strip, 0)
    place = (col_c == lax.broadcasted_iota(jnp.int32, (main, cols), 1)).astype(BF16)

    wet_all = (plan_ref[...] >= 0).astype(F32)
    inv = 1.0 / (jnp.sum(wet_all, axis=(0, 1), keepdims=True) * float(chans * rows * PATCH))
    wet_row = (plan_ref[pl.ds(band, 1), :] >= 0).astype(F32)
    n_cols = wet_row.shape[1]
    at = lax.broadcasted_iota(jnp.int32, (main, n_cols), 1) - sub * tiles
    cc = strip_column((main, n_cols), strip, 0)
    in_tile = (cc >= at * PATCH) & (cc < at * PATCH + PATCH)
    wet_rows = jnp.sum(jnp.where(in_tile, wet_row, 0.0), axis=1, keepdims=True)
    at_x = lax.broadcasted_iota(jnp.int32, (n_cols, cols), 0) - sub * tiles
    x_x = lax.broadcasted_iota(jnp.int32, (n_cols, cols), 1)
    in_x = ((x_x >= at_x * PATCH) & (x_x < at_x * PATCH + PATCH)).astype(BF16)
    wet_x = nn(jnp.broadcast_to(wet_row, (SUBL, n_cols)).astype(BF16), in_x)[0:1]

    for o in range(KSIZE * KSIZE):
        kb_ref[o] = jnp.broadcast_to(dw_ref[o : o + 1, :].astype(F32), (SUBL, width))

    odd = (band & 1) == 1
    for i in range(RIM):
        xa_ref[i] = nt(pick_full, jnp.where(odd, near_ref[i], far_ref[i]))
        xa_ref[i + RIM + rows] = nt(pick_full, jnp.where(odd, far_ref[i], near_ref[i]))
    for i in range(rows):
        xa_ref[i + RIM] = nt(pick, st_ref[i]) + nt(pick_edge, e_ref[i])

    def encode(i, c):
        y = i * RIM
        xa = xa_ref[pl.ds(y, RIM)].reshape(RIM * wmain, chans).astype(BF16)
        enc = nn(xa, wenc_ref[...]).astype(BF16).astype(F32)
        enc_ref[pl.ds(y, RIM)] = enc.reshape(RIM, wmain, width)
        return c

    lax.fori_loop(0, (rows + 2 * RIM) // RIM, encode, 0)

    def conv(y, c):
        for h in range(width // LANES):
            ln = slice(h * LANES, (h + 1) * LANES)
            acc = jnp.zeros((strip, SUBL, LANES), F32)
            for a in range(KSIZE):
                e = enc_ref[y + a, :, ln].reshape(wide, SUBL, LANES)
                for b in range(KSIZE):
                    acc = acc + e[b : b + strip] * kb_ref[a * KSIZE + b, :, ln]
            nrm_ref[y, :, ln] = acc.reshape(main, LANES)
        return c

    lax.fori_loop(0, rows, conv, 0, unroll=2)

    small_ref[...] = jnp.zeros_like(small_ref)
    acc_ref[...] = jnp.zeros_like(acc_ref)
    ge_ref[...] = jnp.zeros_like(ge_ref)
    gain = gain_ref[...]
    group = GROUP
    chunk = group * main
    blocks = hid // width
    wetg = jnp.concatenate([wet_rows] * group, axis=0)

    def mlp(k, loss):
        y0 = k * group
        r0 = pl.multiple_of(k * chunk, chunk)
        v = nrm_ref[pl.ds(y0, group)].reshape(chunk, width)
        cen = v - jnp.mean(v, axis=-1, keepdims=True)
        istd = lax.rsqrt(jnp.mean(cen * cen, axis=-1, keepdims=True) + 1e-06)
        nrm = cen * istd
        nrm_ref[pl.ds(y0, group)] = nrm.reshape(group, main, width)
        istd_ref[...] = jnp.broadcast_to(istd, (chunk, LANES))
        sc_ref[pl.ds(r0, chunk), :] = (nrm * gain).astype(BF16)
        centre = enc_ref[pl.ds(y0 + RIM, group), RIM * SUBL : RIM * SUBL + main, :]
        rs_ref[...] = centre.reshape(chunk, width)

        def up(n, c):
            n0 = pl.multiple_of(n * width, width)
            v = nn(sc_ref[pl.ds(r0, chunk), :], wup_ref[:, pl.ds(n0, width)])
            vv = v * v
            t = jnp.tanh(v * (GELU_A + GELU_B * vv))
            q = 1.0 + t
            soft = 0.5 * v * q
            dg_ref[:, pl.ds(n0, width)] = 0.5 * q + soft * (1.0 - t) * (GELU_A + 3.0 * GELU_B * vv)
            act = soft.astype(BF16)
            act_ref[pl.ds(r0, chunk), pl.ds(n0, width)] = act
            rs_ref[...] += nn(act, wdown_ref[pl.ds(n0, width), :])
            return c

        lax.fori_loop(0, blocks, up, 0, unroll=UNROLL)
        residual = rs_ref[...].astype(BF16)
        base = xa_ref[pl.ds(y0 + RIM, group), RIM * SUBL : RIM * SUBL + main, :]
        pred = base.reshape(chunk, chans) + nt(residual, wdec_ref[...])
        goal = jnp.concatenate([nt(place, tgt_ref[y0 + i]) for i in range(group)], axis=0)
        mis = (pred - goal) * wetg
        for i in range(group):
            back = tn(pred[i * main : (i + 1) * main].astype(BF16), place)
            new_ref[y0 + i] = jnp.where(wet_x > 0.5, back.astype(BF16), st_ref[y0 + i])
        loss = loss + jnp.sum(mis * mis, axis=(0, 1), keepdims=True)
        gout = (mis * (2.0 * inv)).astype(BF16)
        small_ref[AT_DEC : AT_DEC + chans, :] += tn(gout, residual)
        gres = nn(gout, wdec_ref[...]).astype(BF16)
        gr_ref[pl.ds(r0, chunk), :] = gres
        for i in range(group):
            ge_ref[y0 + RIM + i, RIM * SUBL : RIM * SUBL + main, :] = gres[
                i * main : (i + 1) * main
            ].astype(F32)
        gs_ref[...] = jnp.zeros_like(gs_ref)

        def down(n, c):
            n0 = pl.multiple_of(n * width, width)
            ga = nt(gr_ref[pl.ds(r0, chunk), :], wdown_ref[pl.ds(n0, width), :])
            gp = (ga * dg_ref[:, pl.ds(n0, width)]).astype(BF16)
            gp_ref[pl.ds(r0, chunk), pl.ds(n0, width)] = gp
            gs_ref[...] += nt(gp, wup_ref[:, pl.ds(n0, width)])
            return c

        lax.fori_loop(0, blocks, down, 0, unroll=UNROLL)
        gs = gs_ref[...]
        nrm = nrm_ref[pl.ds(y0, group)].reshape(chunk, width)
        prod = gs * nrm
        small_ref[AT_GAIN : AT_GAIN + 1, :] += jnp.sum(prod, axis=0, keepdims=True)
        g = gs * gain
        m1 = jnp.mean(g, axis=-1, keepdims=True)
        m2 = jnp.mean(g * nrm, axis=-1, keepdims=True)
        gc = g - m1 - nrm * m2
        istd = istd_ref[...]
        for h in range(width // LANES):
            ln = slice(h * LANES, (h + 1) * LANES)
            nrm_ref[pl.ds(y0, group), :, ln] = (gc[:, ln] * istd).reshape(group, main, LANES)
        return loss

    loss = lax.fori_loop(0, rows // group, mlp, jnp.zeros((1, 1), F32))
    lane = lax.broadcasted_iota(jnp.int32, (1, width), 1)
    rest = jnp.where(lane == band * lax.axis_size("sub") + sub, loss * inv, 0.0)
    for i in range(3):
        term = rest.astype(BF16).astype(F32)
        small_ref[AT_LOSS + i : AT_LOSS + i + 1, :] = term
        rest = rest - term

    n_piece = keep_ref.shape[0]
    tall = width // n_piece

    def wgrad(n, c):
        n0 = pl.multiple_of(n * width, width)
        g_up = tn(sc_ref[...], gp_ref[:, pl.ds(n0, width)])
        g_down = tn(gr_ref[...], act_ref[:, pl.ds(n0, width)])
        first = sub == 0
        keep = jnp.where(first, g_up, g_down).reshape(n_piece, tall, width)
        send = jnp.where(first, g_down, g_up).reshape(n_piece, tall, width)
        keep_ref[:, 0:tall, pl.ds(n0, width)] = keep
        send_ref[:, 0:tall, pl.ds(n0, width)] = send.astype(BF16)
        return c

    lax.fori_loop(0, blocks, wgrad, 0, unroll=UNROLL)

    def conv_back(y, c):
        for h in range(width // LANES):
            ln = slice(h * LANES, (h + 1) * LANES)
            g = nrm_ref[y, :, ln].reshape(strip, SUBL, LANES)
            for a in range(KSIZE):
                e = enc_ref[y + a, :, ln].reshape(wide, SUBL, LANES)
                out = [ge_ref[y + a, j * SUBL : (j + 1) * SUBL, ln] for j in range(wide)]
                for b in range(KSIZE):
                    o = a * KSIZE + b
                    acc_ref[o, :, ln] += jnp.sum(g * e[b : b + strip], axis=0)
                    k = kb_ref[o, :, ln]
                    for j in range(strip):
                        out[j + b] = out[j + b] + g[j] * k
                for j in range(wide):
                    ge_ref[y + a, j * SUBL : (j + 1) * SUBL, ln] = out[j]
        return c

    lax.fori_loop(0, rows, conv_back, 0)
    high = rows + 2 * RIM
    xa = xa_ref[...].reshape(high * wmain, chans).astype(BF16)
    ge = ge_ref[...].reshape(high * wmain, width).astype(BF16)
    small_ref[0:chans, :] = tn(xa, ge)
    small_ref[AT_DW : AT_DW + KSIZE * KSIZE, :] = jnp.sum(acc_ref[...], axis=1)

    half = SMALL_ROWS // 2
    part = half // n_piece
    flat = part // blocks
    keep = small_ref[pl.ds(pl.multiple_of(sub * half, half), half), :]
    send = small_ref[pl.ds(pl.multiple_of((1 - sub) * half, half), half), :]
    keep = keep.reshape(n_piece, part, width)
    send = send.reshape(n_piece, part, width)
    for q in range(blocks):
        ln = slice(q * width, (q + 1) * width)
        keep_ref[:, tall : tall + flat, ln] = keep[:, q * flat : (q + 1) * flat]
        send_ref[:, tall : tall + flat, ln] = send[:, q * flat : (q + 1) * flat].astype(BF16)


def vmem(n):
    return [pl.BlockSpec(memory_space=pltpu.VMEM) for _ in range(n)]


def grant(mib):
    return pltpu.CompilerParams(vmem_limit_bytes=mib << 20)


def swapped(value, axis, d):
    size = lax.axis_size(axis)
    return lax.ppermute(value, axis, [(i, i ^ d) for i in range(size)])


def pick_kernel(n, keep_ref, recv_ref, own_ref, *out_refs):
    band = lax.axis_index("band")
    own_ref[...] = keep_ref[band] + recv_ref[band].astype(F32)
    for d in range(1, n):
        out_refs[d - 1][...] = (keep_ref[band ^ d] + recv_ref[band ^ d].astype(F32)).astype(BF16)


def add_kernel(n, own_ref, *refs):
    total = own_ref[...]
    for d in range(1, n):
        total = total + refs[d - 1][...].astype(F32)
    refs[n - 1][...] = total.astype(BF16)


def join_kernel(n, *refs):
    band = lax.axis_index("band")
    sem = refs[n + 1]
    copies = [
        pltpu.make_async_copy(refs[d], refs[n].at[band ^ d], sem.at[d]) for d in range(n)
    ]
    for copy in copies:
        copy.start()
    for copy in copies:
        copy.wait()


def spread_kernel(mine_ref, other_ref, up_ref, down_ref, enc_ref, dw_ref, gain_ref, dec_ref, loss_ref, small_ref):
    n, deep, hid = mine_ref.shape
    width = up_ref.shape[0]
    blocks = hid // width
    tall = width // n
    flat = deep - tall
    half = SMALL_ROWS // 2
    sub = lax.axis_index("sub")

    def put(up_from, down_from, first):
        up_ref[...] = up_from[:, 0:tall, :].astype(F32).reshape(width, hid)
        for q in range(blocks):
            ln = slice(q * width, (q + 1) * width)
            down_ref[ln, :] = down_from[:, 0:tall, ln].astype(F32).reshape(width, width).T
            for i, ref in enumerate((up_from, down_from)):
                for p in range(n):
                    r = i * half + p * flat * blocks + q * flat
                    small_ref[r : r + flat, :] = ref[p, tall:deep, ln].astype(F32)

    @pl.when(sub == 0)
    def _():
        put(mine_ref, other_ref, 0)

    @pl.when(sub != 0)
    def _():
        put(other_ref, mine_ref, 1)

    chans = enc_ref.shape[0]
    enc_ref[...] = small_ref[0:chans, :]
    dec_ref[...] = small_ref[AT_DEC : AT_DEC + chans, :]
    dw_ref[...] = small_ref[AT_DW : AT_DW + KSIZE * KSIZE, :]
    gain_ref[...] = small_ref[AT_GAIN : AT_GAIN + 1, :]
    loss_ref[...] = jnp.sum(small_ref[AT_LOSS : AT_LOSS + 3, :], axis=(0, 1), keepdims=True)


def summed(keep, recv, shapes):
    n, deep, hid = keep.shape
    piece = (deep, hid)
    outs = [jax.ShapeDtypeStruct(piece, F32)] + [jax.ShapeDtypeStruct(piece, BF16)] * (n - 1)
    parts = pl.pallas_call(
        lambda *r: pick_kernel(n, *r),
        out_shape=outs, in_specs=vmem(2), out_specs=vmem(n), name="pick",
        compiler_params=grant(12),
    )(keep, recv)
    got = [swapped(parts[d], "band", d) for d in range(n - 1, 0, -1)]
    total = pl.pallas_call(
        lambda *r: add_kernel(n, *r),
        out_shape=jax.ShapeDtypeStruct(piece, BF16),
        in_specs=vmem(n), out_specs=vmem(1)[0], name="add",
        compiler_params=grant(4),
    )(parts[0], *got)
    every = [total] + [swapped(total, "band", d) for d in range(1, n)]
    half = pl.pallas_call(
        lambda *r: join_kernel(n, *r),
        out_shape=jax.ShapeDtypeStruct((n,) + piece, BF16),
        in_specs=vmem(n), out_specs=pl.BlockSpec(memory_space=pl.ANY),
        scratch_shapes=[pltpu.SemaphoreType.DMA((n,))], name="join",
        compiler_params=grant(4),
    )(*every)
    other = swapped(half, "sub", 1)
    return pl.pallas_call(
        spread_kernel,
        out_shape=[jax.ShapeDtypeStruct(s, F32) for s in shapes],
        in_specs=vmem(2), out_specs=vmem(len(shapes)),
        scratch_shapes=[pltpu.VMEM((SMALL_ROWS, shapes[0][0]), F32)],
        name="spread",
        compiler_params=grant(12),
    )(half, other)


def shards(state, target, tile_plan, w_enc, dw_kernel, norm_gain, w_up, w_down, w_dec):
    chans, rows, cols = state.shape
    width = w_enc.shape[1]
    hid = w_up.shape[1]
    main = cols
    wmain = cols + 2 * RIM * SUBL
    high = rows + 2 * RIM
    n_band = lax.axis_size("band")

    st = state.transpose(1, 0, 2)
    tgt = target.transpose(1, 0, 2)
    edges = jnp.concatenate([st[:, :, cols - RIM :], st[:, :, :RIM]], axis=2)
    other = swapped(edges, "sub", 1)
    last = jnp.concatenate([st[rows - RIM :], other[rows - RIM :]], axis=2)
    first = jnp.concatenate([st[:RIM], other[:RIM]], axis=2)
    odd = (lax.axis_index("band") & 1) == 1
    near = lax.ppermute(
        jnp.where(odd, first, last), "band", [(i, i ^ 1) for i in range(n_band)]
    )
    pairs = [(i, i + 1) for i in range(1, n_band - 1, 2)]
    far = lax.ppermute(jnp.where(odd, last, first), "band", pairs + [(j, i) for i, j in pairs])

    cells = rows * main
    chunk = GROUP * main
    n = n_band
    deep = width // n + SMALL_ROWS // 2 * width // (n * hid)
    new, keep, send = pl.pallas_call(
        step_kernel,
        out_shape=[
            jax.ShapeDtypeStruct((rows, chans, cols), BF16),
            jax.ShapeDtypeStruct((n, deep, hid), F32),
            jax.ShapeDtypeStruct((n, deep, hid), BF16),
        ],
        in_specs=vmem(12), out_specs=vmem(3),
        scratch_shapes=[
            pltpu.VMEM((high, wmain, width), F32),
            pltpu.VMEM((high, wmain, chans), F32),
            pltpu.VMEM((KSIZE * KSIZE, SUBL, width), F32),
            pltpu.VMEM((rows, main, width), F32),
            pltpu.VMEM((chunk, LANES), F32),
            pltpu.VMEM((cells, width), BF16),
            pltpu.VMEM((cells, hid), BF16),
            pltpu.VMEM((chunk, hid), F32),
            pltpu.VMEM((cells, hid), BF16),
            pltpu.VMEM((chunk, width), F32),
            pltpu.VMEM((cells, width), BF16),
            pltpu.VMEM((chunk, width), F32),
            pltpu.VMEM((high, wmain, width), F32),
            pltpu.VMEM((KSIZE * KSIZE, SUBL, width), F32),
            pltpu.VMEM((SMALL_ROWS, width), F32),
        ],
        name="step",
        compiler_params=grant(44),
    )(
        tile_plan, st, near, far, other, tgt,
        w_enc, dw_kernel, norm_gain.reshape(1, width), w_up, w_down, w_dec.T,
    )
    new = new.transpose(1, 0, 2)
    recv = swapped(send, "sub", 1)
    new, recv = lax.optimization_barrier((new, recv))
    g_up, g_down, g_enc, g_dw, g_gain, g_dec, loss = summed(
        keep, recv,
        [(width, hid), (hid, width), (chans, width), dw_kernel.shape, (1, width), (chans, width), (1, 1)],
    )
    return (
        new, loss.reshape(1), g_enc, g_dw, g_gain.reshape(width),
        g_up, g_down, g_dec.T,
    )


def solution(mesh):
    return jax.shard_map(
        shards,
        mesh=mesh,
        in_specs=(
            P("groups", "band", "sub"),
            P("groups", "band", "sub"),
            P("groups", None),
            P(),
            P(),
            P(),
            P(),
            P(),
            P(),
        ),
        out_specs=(
            P("groups", "band", "sub"),
            P("groups"),
            P("groups", None),
            P("groups", None),
            P("groups"),
            P("groups", None),
            P("groups", None),
            P("groups", None),
        ),
        check_vma=False,
    )
```

```python
import math

import jax
import jax.numpy as jnp
from jax import lax
from jax.experimental import pallas as pl
from jax.experimental.pallas import tpu as pltpu
from jax.sharding import PartitionSpec as P

F32 = jnp.float32
BF16 = jnp.bfloat16

KSIZE = 7
RIM = KSIZE // 2
PATCH = 12
LANES = 128
SUBL = 8
SMALL_ROWS = 160
GROUP = 12
UNROLL = 4
AT_DW = 80
AT_GAIN = 136
AT_LOSS = 137
GELU_A = math.sqrt(2.0 / math.pi)
GELU_B = GELU_A * 0.044715


def nn(a, b):
    return lax.dot_general(a, b, (((1,), (0,)), ((), ())), preferred_element_type=F32)


def nt(a, b):
    return lax.dot_general(a, b, (((1,), (1,)), ((), ())), preferred_element_type=F32)


def tn(a, b):
    return lax.dot_general(a, b, (((0,), (0,)), ((), ())), preferred_element_type=F32)


QUAD = 4


def reach(d, k, core):
    return d + QUAD * (2 * k + core)


def strip_column(shape, strip, shift):
    r = lax.broadcasted_iota(jnp.int32, shape, 0)
    return (r & (SUBL - 1)) * strip + (r >> 3) - shift


def step_kernel(
    plan_ref, st_ref, near_ref, far_ref, e_ref, tgt_ref,
    wenc_ref, dw_ref, gain_ref, wup_ref, wdown_ref, wdec_ref,
    new_ref, *rest,
):
    keep_refs, send_refs = rest[:QUAD], rest[QUAD : 2 * QUAD]
    enc_ref, nrm_ref, gr_ref, xa_ref, gl_ref = rest[2 * QUAD : 2 * QUAD + 5]
    kb_ref, istd_ref, act_ref, dg_ref, gp_ref, gs_ref, sc_ref, rs_ref, dec_ref, all_ref = rest[
        2 * QUAD + 5 :
    ]
    rows, chans, cols = st_ref.shape
    width = wenc_ref.shape[1]
    hid = wup_ref.shape[1]
    strip = cols // SUBL
    wide = strip + 2 * RIM
    main = strip * SUBL
    wmain = wide * SUBL
    band = lax.axis_index("band")
    sub = lax.axis_index("sub")
    tiles = cols // PATCH

    col_w = strip_column((wmain, cols), strip, RIM)
    pick = (col_w == lax.broadcasted_iota(jnp.int32, (wmain, cols), 1)).astype(BF16)
    edge = lax.broadcasted_iota(jnp.int32, (wmain, 2 * RIM), 1)
    edge_col = jnp.where(edge < RIM, edge - RIM, edge - RIM + cols)
    pick_edge = (strip_column((wmain, 2 * RIM), strip, RIM) == edge_col).astype(BF16)
    full = lax.broadcasted_iota(jnp.int32, (wmain, cols + 2 * RIM), 1)
    left = full - cols - RIM
    full_col = jnp.where(full < cols, full, jnp.where(left < 0, left, left + cols))
    pick_full = (strip_column(full.shape, strip, RIM) == full_col).astype(BF16)
    col_c = strip_column((main, cols), strip, 0)
    place = (col_c == lax.broadcasted_iota(jnp.int32, (main, cols), 1)).astype(BF16)

    wet_all = (plan_ref[...] >= 0).astype(F32)
    inv = 1.0 / (jnp.sum(wet_all, axis=(0, 1), keepdims=True) * float(chans * rows * PATCH))
    wet_row = (plan_ref[pl.ds(band, 1), :] >= 0).astype(F32)
    n_cols = wet_row.shape[1]
    at = lax.broadcasted_iota(jnp.int32, (main, n_cols), 1) - sub * tiles
    cc = strip_column((main, n_cols), strip, 0)
    in_tile = (cc >= at * PATCH) & (cc < at * PATCH + PATCH)
    wet_rows = jnp.sum(jnp.where(in_tile, wet_row, 0.0), axis=1, keepdims=True)
    at_x = lax.broadcasted_iota(jnp.int32, (n_cols, cols), 0) - sub * tiles
    x_x = lax.broadcasted_iota(jnp.int32, (n_cols, cols), 1)
    in_x = ((x_x >= at_x * PATCH) & (x_x < at_x * PATCH + PATCH)).astype(BF16)
    wet_x = nn(jnp.broadcast_to(wet_row, (SUBL, n_cols)).astype(BF16), in_x)[0:1]

    for o in range(KSIZE * KSIZE):
        kb_ref[o] = jnp.broadcast_to(dw_ref[o : o + 1, :].astype(F32), (SUBL, width))

    odd = (band & 1) == 1
    for i in range(RIM):
        xa_ref[i] = nt(pick_full, jnp.where(odd, near_ref[i], far_ref[i]))
        xa_ref[i + RIM + rows] = nt(pick_full, jnp.where(odd, far_ref[i], near_ref[i]))
    for i in range(rows):
        xa_ref[i + RIM] = nt(pick, st_ref[i]) + nt(pick_edge, e_ref[i])

    def encode(i, c):
        y = i * RIM
        xa = xa_ref[pl.ds(y, RIM)].reshape(RIM * wmain, chans).astype(BF16)
        enc = nn(xa, wenc_ref[...]).astype(BF16).astype(F32)
        enc_ref[pl.ds(y, RIM)] = enc.reshape(RIM, wmain, width)
        return c

    lax.fori_loop(0, (rows + 2 * RIM) // RIM, encode, 0)

    def conv(y, c):
        for h in range(width // LANES):
            ln = slice(h * LANES, (h + 1) * LANES)
            acc = jnp.zeros((strip, SUBL, LANES), F32)
            for a in range(KSIZE):
                e = enc_ref[y + a, :, ln].reshape(wide, SUBL, LANES)
                for b in range(KSIZE):
                    acc = acc + e[b : b + strip] * kb_ref[a * KSIZE + b, :, ln]
            nrm_ref[y, :, ln] = acc.reshape(main, LANES)
        return c

    lax.fori_loop(0, rows, conv, 0, unroll=2)

    dec_ref[...] = jnp.zeros_like(dec_ref)
    gl_ref[...] = jnp.zeros_like(gl_ref)
    gain = gain_ref[...]
    group = GROUP
    chunk = group * main
    blocks = hid // width
    wetg = jnp.concatenate([wet_rows] * group, axis=0)

    def mlp(k, loss):
        y0 = k * group
        r0 = pl.multiple_of(k * chunk, chunk)
        v = nrm_ref[pl.ds(y0, group)].reshape(chunk, width)
        cen = v - jnp.mean(v, axis=-1, keepdims=True)
        istd = lax.rsqrt(jnp.mean(cen * cen, axis=-1, keepdims=True) + 1e-06)
        nrm = cen * istd
        nrm_ref[pl.ds(y0, group)] = nrm.reshape(group, main, width)
        istd_ref[...] = jnp.broadcast_to(istd, (chunk, LANES))
        sc_ref[pl.ds(r0, chunk), :] = (nrm * gain).astype(BF16)
        centre = enc_ref[pl.ds(y0 + RIM, group), RIM * SUBL : RIM * SUBL + main, :]
        rs_ref[...] = centre.reshape(chunk, width)

        def up(n, c):
            n0 = pl.multiple_of(n * width, width)
            v = nn(sc_ref[pl.ds(r0, chunk), :], wup_ref[:, pl.ds(n0, width)])
            vv = v * v
            t = jnp.tanh(v * (GELU_A + GELU_B * vv))
            q = 1.0 + t
            soft = 0.5 * v * q
            dg_ref[:, pl.ds(n0, width)] = 0.5 * q + soft * (1.0 - t) * (GELU_A + 3.0 * GELU_B * vv)
            act = soft.astype(BF16)
            act_ref[pl.ds(r0, chunk), pl.ds(n0, width)] = act
            rs_ref[...] += nn(act, wdown_ref[pl.ds(n0, width), :])
            return c

        lax.fori_loop(0, blocks, up, 0, unroll=UNROLL)
        residual = rs_ref[...].astype(BF16)
        base = xa_ref[pl.ds(y0 + RIM, group), RIM * SUBL : RIM * SUBL + main, :]
        pred = base.reshape(chunk, chans) + nt(residual, wdec_ref[...])
        goal = jnp.concatenate([nt(place, tgt_ref[y0 + i]) for i in range(group)], axis=0)
        mis = (pred - goal) * wetg
        for i in range(group):
            back = tn(pred[i * main : (i + 1) * main].astype(BF16), place)
            new_ref[y0 + i] = jnp.where(wet_x > 0.5, back.astype(BF16), st_ref[y0 + i])
        loss = loss + jnp.sum(mis * mis, axis=(0, 1), keepdims=True)
        gout = (mis * (2.0 * inv)).astype(BF16)
        dec_ref[0:chans, :] += tn(gout, residual)
        gres = nn(gout, wdec_ref[...]).astype(BF16)
        gr_ref[pl.ds(r0, chunk), :] = gres
        gs_ref[...] = jnp.zeros_like(gs_ref)

        def down(n, c):
            n0 = pl.multiple_of(n * width, width)
            ga = nt(gr_ref[pl.ds(r0, chunk), :], wdown_ref[pl.ds(n0, width), :])
            gp = (ga * dg_ref[:, pl.ds(n0, width)]).astype(BF16)
            gp_ref[pl.ds(r0, chunk), pl.ds(n0, width)] = gp
            gs_ref[...] += nt(gp, wup_ref[:, pl.ds(n0, width)])
            return c

        lax.fori_loop(0, blocks, down, 0, unroll=UNROLL)
        gs = gs_ref[...]
        nrm = nrm_ref[pl.ds(y0, group)].reshape(chunk, width)
        prod = gs * nrm
        gl_ref[0:1, :] += jnp.sum(prod, axis=0, keepdims=True)
        g = gs * gain
        m1 = jnp.mean(g, axis=-1, keepdims=True)
        m2 = jnp.mean(g * nrm, axis=-1, keepdims=True)
        gc = g - m1 - nrm * m2
        istd = istd_ref[...]
        for h in range(width // LANES):
            ln = slice(h * LANES, (h + 1) * LANES)
            nrm_ref[pl.ds(y0, group), :, ln] = (gc[:, ln] * istd).reshape(group, main, LANES)
        return loss

    loss = lax.fori_loop(0, rows // group, mlp, jnp.zeros((1, 1), F32))
    lane = lax.broadcasted_iota(jnp.int32, (1, width), 1)
    rest = jnp.where(lane == band * lax.axis_size("sub") + sub, loss * inv, 0.0)
    for i in range(3):
        term = rest.astype(BF16).astype(F32)
        gl_ref[1 + i : 2 + i, :] = term
        rest = rest - term

    n_piece, tall, _ = all_ref.shape

    def wgrad(n, c):
        n0 = pl.multiple_of(n * width, width)
        g_up = tn(sc_ref[...], gp_ref[:, pl.ds(n0, width)])
        g_down = tn(gr_ref[...], act_ref[:, pl.ds(n0, width)])
        all_ref[:, :, pl.ds(n0, width)] = g_up.reshape(n_piece, tall, width)
        all_ref[:, :, pl.ds(pl.multiple_of(hid + n0, width), width)] = g_down.reshape(
            n_piece, tall, width
        )
        return c

    lax.fori_loop(0, blocks, wgrad, 0, unroll=UNROLL)

    all_ref[:, :, 2 * hid :] = dec_ref[...].T.reshape(n_piece, tall, LANES)
    for d in range(QUAD):
        for k in range(n_piece // (2 * QUAD)):
            keep_refs[d][k] = all_ref[band ^ reach(d, k, sub)]
            send_refs[d][k] = all_ref[band ^ reach(d, k, 1 - sub)].astype(BF16)


def back_kernel(
    h, gate_ref, enc_ref, gconv_ref, gr_ref, xa_ref, dw_ref, gl_ref, out_ref, kb_ref, acc_ref, ge_ref
):
    rows, main, _ = gconv_ref.shape
    high, wmain, chans = xa_ref.shape
    strip = main // SUBL
    wide = wmain // SUBL
    ln = slice(h * LANES, (h + 1) * LANES)
    for o in range(KSIZE * KSIZE):
        kb_ref[o] = jnp.broadcast_to(dw_ref[o : o + 1, ln].astype(F32), (SUBL, LANES))
    acc_ref[...] = jnp.zeros_like(acc_ref)
    ge_ref[...] = jnp.zeros_like(ge_ref)
    centre = gr_ref[:, ln].astype(F32).reshape(rows, main, LANES)
    ge_ref[RIM : RIM + rows, RIM * SUBL : RIM * SUBL + main, :] = centre

    def conv_back(y, c):
        g = gconv_ref[y, :, ln].reshape(strip, SUBL, LANES)
        for a in range(KSIZE):
            e = enc_ref[y + a, :, ln].reshape(wide, SUBL, LANES)
            out = [ge_ref[y + a, j * SUBL : (j + 1) * SUBL, :] for j in range(wide)]
            for b in range(KSIZE):
                o = a * KSIZE + b
                acc_ref[o] += jnp.sum(g * e[b : b + strip], axis=0)
                k = kb_ref[o]
                for j in range(strip):
                    out[j + b] = out[j + b] + g[j] * k
            for j in range(wide):
                ge_ref[y + a, j * SUBL : (j + 1) * SUBL, :] = out[j]
        return c

    lax.fori_loop(0, rows, conv_back, 0)
    xa = xa_ref[...].reshape(high * wmain, chans).astype(BF16)
    ge = ge_ref[...].reshape(high * wmain, LANES).astype(BF16)
    out_ref[...] = jnp.zeros_like(out_ref)
    out_ref[0:chans, :] = tn(xa, ge)
    out_ref[AT_DW : AT_DW + KSIZE * KSIZE, :] = jnp.sum(acc_ref[...], axis=1)
    out_ref[AT_GAIN : AT_GAIN + SUBL, :] = gl_ref[:, ln]


def vmem(n):
    return [pl.BlockSpec(memory_space=pltpu.VMEM) for _ in range(n)]


def grant(mib):
    return pltpu.CompilerParams(vmem_limit_bytes=mib << 20)


def swapped(value, axis, d):
    size = lax.axis_size(axis)
    return lax.ppermute(value, axis, [(i, i ^ d) for i in range(size)])


def between_blocks(value, g, gather):
    n = lax.axis_size("band")
    moves = [(b * 2 + (g & 1), (b ^ (QUAD * g)) * 2) for b in range(n)]
    if gather:
        moves = [(j, i) for i, j in moves]
    return lax.ppermute(value, ("band", "sub"), moves)


def pick_kernel(keep_ref, recv_ref, out_ref):
    out_ref[...] = (keep_ref[...] + recv_ref[...].astype(F32)).astype(out_ref.dtype)


def block_kernel(gate_ref, own_ref, *refs):
    base_ref, out_refs = refs[QUAD - 1], refs[QUAD:]
    total = own_ref[...]
    for ref in refs[: QUAD - 1]:
        total = total + ref[...].astype(F32)
    base_ref[...] = jnp.where(lax.axis_index("sub") == 0, total[0], 0.0)
    for g in range(1, len(out_refs) + 1):
        out_refs[g - 1][...] = total[g // 2].astype(BF16)


def total_kernel(gate_ref, base_ref, *refs):
    total = base_ref[...]
    for ref in refs[:-1]:
        total = total + ref[...].astype(F32)
    refs[-1][...] = total.astype(BF16)


def hold_kernel(small_ref, *refs):
    out_ref = refs[-1]
    first = lax.axis_index("sub") == 0
    slots, tall, _ = out_ref.shape
    deep = refs[0].shape[1]
    for k in range(slots):
        out_ref[k, :, 0:deep] = jnp.where(first, refs[2 * k][...], refs[2 * k + 1][...])
    high = slots * tall
    for i in range(small_ref.shape[0] // high):
        at = deep + i * LANES
        block = small_ref[i * high : (i + 1) * high, :]
        out_ref[:, :, at : at + LANES] = block.reshape(slots, tall, LANES)


def halve_kernel(a_ref, b_ref, keep_ref, send_ref):
    first = lax.axis_index("sub") == 0
    a, b = a_ref[...], b_ref[...]
    keep_ref[...] = jnp.where(first, a, b)
    send_ref[...] = jnp.where(first, b, a).astype(BF16)


def pair_kernel(mine_ref, other_ref, out_ref):
    out_ref[...] = (mine_ref[...].astype(F32) + other_ref[...].astype(F32)).astype(BF16)


def spread_kernel(*refs):
    mine, other = refs[:QUAD], refs[QUAD : 2 * QUAD]
    up_ref, down_ref, enc_ref, dw_ref, gain_ref, dec_ref, loss_ref = refs[2 * QUAD : -3]
    small_ref, turned_ref, dec_t_ref = refs[-3:]
    slots, tall, _ = mine[0].shape
    width, hid = up_ref.shape
    chans = enc_ref.shape[0]
    band = lax.axis_index("band")
    sub = lax.axis_index("sub")
    deep = 2 * hid + LANES
    high = slots * tall
    for side, core in ((mine, sub), (other, 1 - sub)):
        for d in range(QUAD):
            for k in range(slots):
                at = pl.multiple_of((band ^ reach(d, k, core)) * tall, tall)
                rows = pl.ds(at, tall)
                up_ref[rows, :] = side[d][k, :, 0:hid].astype(F32)
                turned_ref[rows, :] = side[d][k, :, hid : 2 * hid].astype(F32)
                dec_t_ref[rows, :] = side[d][k, :, 2 * hid : deep].astype(F32)
        for i in range(SMALL_ROWS // high):
            ln = slice(deep + i * LANES, deep + (i + 1) * LANES)
            a, b, c, e = [side[d][:, :, ln].astype(F32) for d in range(QUAD)]
            small_ref[i * high : (i + 1) * high, pl.ds(pl.multiple_of(core * LANES, LANES), LANES)] = (
                ((a + b) + (c + e)).reshape(high, LANES)
            )
    for q in range(hid // width):
        ln = slice(q * width, (q + 1) * width)
        down_ref[ln, :] = turned_ref[:, ln].T
    enc_ref[...] = small_ref[0:chans, :]
    dec_ref[...] = dec_t_ref[...].T[0:chans, :]
    dw_ref[...] = small_ref[AT_DW : AT_DW + KSIZE * KSIZE, :]
    gain_ref[...] = small_ref[AT_GAIN : AT_GAIN + 1, :]
    loss_ref[...] = jnp.sum(small_ref[AT_LOSS : AT_LOSS + 3, :], axis=(0, 1), keepdims=True)


def local(body, out_shape, mib, name, *args, gates=(), scratch=(), cost=None):
    many = isinstance(out_shape, (list, tuple))
    return pl.pallas_call(
        body,
        out_shape=out_shape,
        in_specs=[pl.BlockSpec(memory_space=pl.ANY) for _ in gates] + vmem(len(args)),
        out_specs=vmem(len(out_shape)) if many else vmem(1)[0],
        scratch_shapes=list(scratch), name=name, compiler_params=grant(mib), cost_estimate=cost,
    )(*gates, *args)


def summed(keep, send, inner, shapes):
    enc, gconv, gr, xa, dw_kernel, gl = inner
    slots, tall, deep = keep[0].shape
    blocks = 2 * slots
    n = lax.axis_size("band")
    piece = (tall, deep)
    slab = (slots,) + piece
    high, wmain, _ = xa.shape

    def back(h, gate):
        return local(
            lambda *r: back_kernel(h, *r),
            jax.ShapeDtypeStruct((SMALL_ROWS, LANES), F32), 10, f"back{h}",
            enc, gconv, gr, xa, dw_kernel, gl,
            gates=(gate,),
            scratch=[
                pltpu.VMEM((KSIZE * KSIZE, SUBL, LANES), F32),
                pltpu.VMEM((KSIZE * KSIZE, SUBL, LANES), F32),
                pltpu.VMEM((high, wmain, LANES), F32),
            ],
            cost=pl.CostEstimate(flops=3_000_000_000, bytes_accessed=18_000_000, transcendentals=0),
        )

    got = []
    for d in range(QUAD - 1, -1, -1):
        shape = jax.ShapeDtypeStruct(slab, BF16 if d else F32)
        part = local(pick_kernel, shape, 6, f"pick{d}", keep[d], swapped(send[d], "sub", 1))
        got.append(swapped(part, "band", d) if d else part)
    small_a = back(0, got[-1])
    base, *far = local(
        block_kernel,
        [jax.ShapeDtypeStruct(piece, F32)] + [jax.ShapeDtypeStruct(piece, BF16)] * (blocks - 1),
        8, "block", got[-1], *got[:-1], gates=(small_a,),
    )
    got = [between_blocks(far[g - 1], g, False) for g in range(1, blocks)]
    small_b = back(1, far[0])
    total = local(
        total_kernel, jax.ShapeDtypeStruct(piece, BF16), 4, "total", base, *got, gates=(small_b,)
    )
    half = (SMALL_ROWS, LANES)
    s_keep, s_send = local(
        halve_kernel,
        [jax.ShapeDtypeStruct(half, F32), jax.ShapeDtypeStruct(half, BF16)],
        4, "halve", small_a, small_b,
    )
    small = local(
        pick_kernel, jax.ShapeDtypeStruct(half, BF16), 4, "chip", s_keep, swapped(s_send, "sub", 1)
    )
    got = [between_blocks(total, g, True) for g in range(1, blocks)]
    step = QUAD
    while step < n:
        small = local(
            pair_kernel, jax.ShapeDtypeStruct(half, BF16), 4, "pair",
            small, swapped(small, "band", step),
        )
        step *= 2
    hold = local(
        hold_kernel,
        jax.ShapeDtypeStruct((slots, tall, deep + SMALL_ROWS // (slots * tall) * LANES), BF16),
        4, "hold", small, total, *got,
    )
    mine = [hold] + [swapped(hold, "band", d) for d in range(1, QUAD)]
    other = [swapped(value, "sub", 1) for value in mine]
    width, hid = shapes[0]
    return local(
        spread_kernel, [jax.ShapeDtypeStruct(s, F32) for s in shapes], 16, "spread",
        *mine, *other,
        scratch=[
            pltpu.VMEM((SMALL_ROWS, width), F32),
            pltpu.VMEM((width, hid), F32),
            pltpu.VMEM((width, LANES), F32),
        ],
    )


def shards(state, target, tile_plan, w_enc, dw_kernel, norm_gain, w_up, w_down, w_dec):
    chans, rows, cols = state.shape
    width = w_enc.shape[1]
    hid = w_up.shape[1]
    main = cols
    wmain = cols + 2 * RIM * SUBL
    high = rows + 2 * RIM
    n_band = lax.axis_size("band")

    st = state.transpose(1, 0, 2)
    tgt = target.transpose(1, 0, 2)
    edges = jnp.concatenate([st[:, :, cols - RIM :], st[:, :, :RIM]], axis=2)
    other = swapped(edges, "sub", 1)
    last = jnp.concatenate([st[rows - RIM :], other[rows - RIM :]], axis=2)
    first = jnp.concatenate([st[:RIM], other[:RIM]], axis=2)
    odd = (lax.axis_index("band") & 1) == 1
    near = lax.ppermute(
        jnp.where(odd, first, last), "band", [(i, i ^ 1) for i in range(n_band)]
    )
    pairs = [(i, i + 1) for i in range(1, n_band - 1, 2)]
    far = lax.ppermute(jnp.where(odd, last, first), "band", pairs + [(j, i) for i, j in pairs])

    cells = rows * main
    chunk = GROUP * main
    n = n_band
    tall = width // n
    deep = 2 * hid + LANES
    slab = (n // (2 * QUAD), tall, deep)
    new, *rest = pl.pallas_call(
        step_kernel,
        out_shape=[
            jax.ShapeDtypeStruct((rows, chans, cols), BF16),
            *[jax.ShapeDtypeStruct(slab, F32)] * QUAD,
            *[jax.ShapeDtypeStruct(slab, BF16)] * QUAD,
            jax.ShapeDtypeStruct((high, wmain, width), F32),
            jax.ShapeDtypeStruct((rows, main, width), F32),
            jax.ShapeDtypeStruct((cells, width), BF16),
            jax.ShapeDtypeStruct((high, wmain, chans), F32),
            jax.ShapeDtypeStruct((SUBL, width), F32),
        ],
        in_specs=vmem(12), out_specs=vmem(6 + 2 * QUAD),
        scratch_shapes=[
            pltpu.VMEM((KSIZE * KSIZE, SUBL, width), F32),
            pltpu.VMEM((chunk, LANES), F32),
            pltpu.VMEM((cells, hid), BF16),
            pltpu.VMEM((chunk, hid), F32),
            pltpu.VMEM((cells, hid), BF16),
            pltpu.VMEM((chunk, width), F32),
            pltpu.VMEM((cells, width), BF16),
            pltpu.VMEM((chunk, width), F32),
            pltpu.VMEM((LANES, width), F32),
            pltpu.VMEM((n, tall, deep), F32),
        ],
        name="step",
        compiler_params=grant(36),
    )(
        tile_plan, st, near, far, other, tgt,
        w_enc, dw_kernel, norm_gain.reshape(1, width), w_up, w_down, w_dec.T,
    )
    g_up, g_down, g_enc, g_dw, g_gain, g_dec, loss = summed(
        rest[:QUAD], rest[QUAD : 2 * QUAD],
        (*rest[2 * QUAD : 2 * QUAD + 4], dw_kernel, rest[2 * QUAD + 4]),
        [(width, hid), (hid, width), (chans, width), dw_kernel.shape, (1, width), (chans, width), (1, 1)],
    )
    return (
        new.transpose(1, 0, 2), loss.reshape(1), g_enc, g_dw, g_gain.reshape(width),
        g_up, g_down, g_dec.T,
    )


def solution(mesh):
    return jax.shard_map(
        shards,
        mesh=mesh,
        in_specs=(
            P("groups", "band", "sub"),
            P("groups", "band", "sub"),
            P("groups", None),
            P(),
            P(),
            P(),
            P(),
            P(),
            P(),
        ),
        out_specs=(
            P("groups", "band", "sub"),
            P("groups"),
            P("groups", None),
            P("groups", None),
            P("groups"),
            P("groups", None),
            P("groups", None),
            P("groups", None),
        ),
        check_vma=False,
    )
```

```python
import math

import jax
import jax.numpy as jnp
from jax import lax
from jax.experimental import pallas as pl
from jax.experimental.pallas import tpu as pltpu
from jax.sharding import PartitionSpec as P

F32 = jnp.float32
BF16 = jnp.bfloat16

KSIZE = 7
RIM = KSIZE // 2
PATCH = 12
LANES = 128
SUBL = 8
SMALL_ROWS = 256
GROUP = 12
UNROLL = 4
AT_DEC = 80
AT_DW = 160
AT_GAIN = 216
AT_LOSS = 217
GELU_A = math.sqrt(2.0 / math.pi)
GELU_B = GELU_A * 0.044715


def nn(a, b):
    return lax.dot_general(a, b, (((1,), (0,)), ((), ())), preferred_element_type=F32)


def nt(a, b):
    return lax.dot_general(a, b, (((1,), (1,)), ((), ())), preferred_element_type=F32)


def tn(a, b):
    return lax.dot_general(a, b, (((0,), (0,)), ((), ())), preferred_element_type=F32)


QUAD = 4


def reach(d, g):
    return d + QUAD * g


def strip_column(shape, strip, shift):
    r = lax.broadcasted_iota(jnp.int32, shape, 0)
    return (r & (SUBL - 1)) * strip + (r >> 3) - shift


def step_kernel(
    plan_ref, st_ref, near_ref, far_ref, e_ref, tgt_ref,
    wenc_ref, dw_ref, gain_ref, wup_ref, wdown_ref, wdec_ref,
    new_ref, *rest,
):
    keep_refs, send_refs = rest[:QUAD], rest[QUAD : 2 * QUAD]
    enc_ref, nrm_ref, gr_ref, xa_ref, gl_ref, dec_ref = rest[2 * QUAD : 2 * QUAD + 6]
    kb_ref, istd_ref, act_ref, dg_ref, gp_ref, gs_ref, sc_ref, rs_ref, all_ref = rest[
        2 * QUAD + 6 :
    ]
    rows, chans, cols = st_ref.shape
    width = wenc_ref.shape[1]
    hid = wup_ref.shape[1]
    strip = cols // SUBL
    wide = strip + 2 * RIM
    main = strip * SUBL
    wmain = wide * SUBL
    band = lax.axis_index("band")
    sub = lax.axis_index("sub")
    tiles = cols // PATCH

    col_w = strip_column((wmain, cols), strip, RIM)
    pick = (col_w == lax.broadcasted_iota(jnp.int32, (wmain, cols), 1)).astype(BF16)
    edge = lax.broadcasted_iota(jnp.int32, (wmain, 2 * RIM), 1)
    edge_col = jnp.where(edge < RIM, edge - RIM, edge - RIM + cols)
    pick_edge = (strip_column((wmain, 2 * RIM), strip, RIM) == edge_col).astype(BF16)
    full = lax.broadcasted_iota(jnp.int32, (wmain, cols + 2 * RIM), 1)
    left = full - cols - RIM
    full_col = jnp.where(full < cols, full, jnp.where(left < 0, left, left + cols))
    pick_full = (strip_column(full.shape, strip, RIM) == full_col).astype(BF16)
    col_c = strip_column((main, cols), strip, 0)
    place = (col_c == lax.broadcasted_iota(jnp.int32, (main, cols), 1)).astype(BF16)

    wet_all = (plan_ref[...] >= 0).astype(F32)
    inv = 1.0 / (jnp.sum(wet_all, axis=(0, 1), keepdims=True) * float(chans * rows * PATCH))
    wet_row = (plan_ref[pl.ds(band, 1), :] >= 0).astype(F32)
    n_cols = wet_row.shape[1]
    at = lax.broadcasted_iota(jnp.int32, (main, n_cols), 1) - sub * tiles
    cc = strip_column((main, n_cols), strip, 0)
    in_tile = (cc >= at * PATCH) & (cc < at * PATCH + PATCH)
    wet_rows = jnp.sum(jnp.where(in_tile, wet_row, 0.0), axis=1, keepdims=True)
    at_x = lax.broadcasted_iota(jnp.int32, (n_cols, cols), 0) - sub * tiles
    x_x = lax.broadcasted_iota(jnp.int32, (n_cols, cols), 1)
    in_x = ((x_x >= at_x * PATCH) & (x_x < at_x * PATCH + PATCH)).astype(BF16)
    wet_x = nn(jnp.broadcast_to(wet_row, (SUBL, n_cols)).astype(BF16), in_x)[0:1]

    for o in range(KSIZE * KSIZE):
        kb_ref[o] = jnp.broadcast_to(dw_ref[o : o + 1, :].astype(F32), (SUBL, width))

    odd = (band & 1) == 1
    for i in range(RIM):
        xa_ref[i] = nt(pick_full, jnp.where(odd, near_ref[i], far_ref[i]))
        xa_ref[i + RIM + rows] = nt(pick_full, jnp.where(odd, far_ref[i], near_ref[i]))
    for i in range(rows):
        xa_ref[i + RIM] = nt(pick, st_ref[i]) + nt(pick_edge, e_ref[i])

    def encode(i, c):
        y = i * RIM
        xa = xa_ref[pl.ds(y, RIM)].reshape(RIM * wmain, chans).astype(BF16)
        enc = nn(xa, wenc_ref[...]).astype(BF16).astype(F32)
        enc_ref[pl.ds(y, RIM)] = enc.reshape(RIM, wmain, width)
        return c

    lax.fori_loop(0, (rows + 2 * RIM) // RIM, encode, 0)

    def conv(y, c):
        for h in range(width // LANES):
            ln = slice(h * LANES, (h + 1) * LANES)
            acc = jnp.zeros((strip, SUBL, LANES), F32)
            for a in range(KSIZE):
                e = enc_ref[y + a, :, ln].reshape(wide, SUBL, LANES)
                for b in range(KSIZE):
                    acc = acc + e[b : b + strip] * kb_ref[a * KSIZE + b, :, ln]
            nrm_ref[y, :, ln] = acc.reshape(main, LANES)
        return c

    lax.fori_loop(0, rows, conv, 0, unroll=2)

    dec_ref[...] = jnp.zeros_like(dec_ref)
    gl_ref[...] = jnp.zeros_like(gl_ref)
    gain = gain_ref[...]
    group = GROUP
    chunk = group * main
    blocks = hid // width
    wetg = jnp.concatenate([wet_rows] * group, axis=0)

    def mlp(k, loss):
        y0 = k * group
        r0 = pl.multiple_of(k * chunk, chunk)
        v = nrm_ref[pl.ds(y0, group)].reshape(chunk, width)
        cen = v - jnp.mean(v, axis=-1, keepdims=True)
        istd = lax.rsqrt(jnp.mean(cen * cen, axis=-1, keepdims=True) + 1e-06)
        nrm = cen * istd
        nrm_ref[pl.ds(y0, group)] = nrm.reshape(group, main, width)
        istd_ref[...] = jnp.broadcast_to(istd, (chunk, LANES))
        sc_ref[pl.ds(r0, chunk), :] = (nrm * gain).astype(BF16)
        centre = enc_ref[pl.ds(y0 + RIM, group), RIM * SUBL : RIM * SUBL + main, :]
        rs_ref[...] = centre.reshape(chunk, width)

        def up(n, c):
            n0 = pl.multiple_of(n * width, width)
            v = nn(sc_ref[pl.ds(r0, chunk), :], wup_ref[:, pl.ds(n0, width)])
            vv = v * v
            t = jnp.tanh(v * (GELU_A + GELU_B * vv))
            q = 1.0 + t
            soft = 0.5 * v * q
            dg_ref[:, pl.ds(n0, width)] = 0.5 * q + soft * (1.0 - t) * (GELU_A + 3.0 * GELU_B * vv)
            act = soft.astype(BF16)
            act_ref[pl.ds(r0, chunk), pl.ds(n0, width)] = act
            rs_ref[...] += nn(act, wdown_ref[pl.ds(n0, width), :])
            return c

        lax.fori_loop(0, blocks, up, 0, unroll=UNROLL)
        residual = rs_ref[...].astype(BF16)
        base = xa_ref[pl.ds(y0 + RIM, group), RIM * SUBL : RIM * SUBL + main, :]
        pred = base.reshape(chunk, chans) + nt(residual, wdec_ref[...])
        goal = jnp.concatenate([nt(place, tgt_ref[y0 + i]) for i in range(group)], axis=0)
        mis = (pred - goal) * wetg
        for i in range(group):
            back = tn(pred[i * main : (i + 1) * main].astype(BF16), place)
            new_ref[y0 + i] = jnp.where(wet_x > 0.5, back.astype(BF16), st_ref[y0 + i])
        loss = loss + jnp.sum(mis * mis, axis=(0, 1), keepdims=True)
        gout = (mis * (2.0 * inv)).astype(BF16)
        dec_ref[0:chans, :] += tn(gout, residual)
        gres = nn(gout, wdec_ref[...]).astype(BF16)
        gr_ref[pl.ds(r0, chunk), :] = gres
        gs_ref[...] = jnp.zeros_like(gs_ref)

        def down(n, c):
            n0 = pl.multiple_of(n * width, width)
            ga = nt(gr_ref[pl.ds(r0, chunk), :], wdown_ref[pl.ds(n0, width), :])
            gp = (ga * dg_ref[:, pl.ds(n0, width)]).astype(BF16)
            gp_ref[pl.ds(r0, chunk), pl.ds(n0, width)] = gp
            gs_ref[...] += nt(gp, wup_ref[:, pl.ds(n0, width)])
            return c

        lax.fori_loop(0, blocks, down, 0, unroll=UNROLL)
        gs = gs_ref[...]
        nrm = nrm_ref[pl.ds(y0, group)].reshape(chunk, width)
        prod = gs * nrm
        gl_ref[0:1, :] += jnp.sum(prod, axis=0, keepdims=True)
        g = gs * gain
        m1 = jnp.mean(g, axis=-1, keepdims=True)
        m2 = jnp.mean(g * nrm, axis=-1, keepdims=True)
        gc = g - m1 - nrm * m2
        istd = istd_ref[...]
        for h in range(width // LANES):
            ln = slice(h * LANES, (h + 1) * LANES)
            nrm_ref[pl.ds(y0, group), :, ln] = (gc[:, ln] * istd).reshape(group, main, LANES)
        return loss

    loss = lax.fori_loop(0, rows // group, mlp, jnp.zeros((1, 1), F32))
    lane = lax.broadcasted_iota(jnp.int32, (1, width), 1)
    rest = jnp.where(lane == band * lax.axis_size("sub") + sub, loss * inv, 0.0)
    for i in range(3):
        term = rest.astype(BF16).astype(F32)
        gl_ref[1 + i : 2 + i, :] = term
        rest = rest - term

    n_piece, tall, _ = all_ref.shape

    def wgrad(n, c):
        n0 = pl.multiple_of(n * width, width)
        g_up = tn(sc_ref[...], gp_ref[:, pl.ds(n0, width)])
        g_down = tn(gr_ref[...], act_ref[:, pl.ds(n0, width)])
        all_ref[:, :, pl.ds(n0, width)] = g_up.reshape(n_piece, tall, width)
        all_ref[:, :, pl.ds(pl.multiple_of(hid + n0, width), width)] = g_down.reshape(
            n_piece, tall, width
        )
        return c

    lax.fori_loop(0, blocks, wgrad, 0, unroll=UNROLL)

    mine = pl.ds(pl.multiple_of(sub * hid, hid), hid)
    theirs = pl.ds(pl.multiple_of((1 - sub) * hid, hid), hid)
    for d in range(QUAD):
        for g in range(n_piece // QUAD):
            keep_refs[d][g] = all_ref[band ^ reach(d, g), :, mine]
            send_refs[d][g] = all_ref[band ^ reach(d, g), :, theirs].astype(BF16)


def back_kernel(
    h, gate_ref, enc_ref, gconv_ref, gr_ref, xa_ref, dw_ref, gl_ref, dec_ref,
    out_ref, kb_ref, acc_ref, ge_ref,
):
    rows, main, _ = gconv_ref.shape
    high, wmain, chans = xa_ref.shape
    strip = main // SUBL
    wide = wmain // SUBL
    ln = slice(h * LANES, (h + 1) * LANES)
    for o in range(KSIZE * KSIZE):
        kb_ref[o] = jnp.broadcast_to(dw_ref[o : o + 1, ln].astype(F32), (SUBL, LANES))
    acc_ref[...] = jnp.zeros_like(acc_ref)
    ge_ref[...] = jnp.zeros_like(ge_ref)
    centre = gr_ref[:, ln].astype(F32).reshape(rows, main, LANES)
    ge_ref[RIM : RIM + rows, RIM * SUBL : RIM * SUBL + main, :] = centre

    def conv_back(y, c):
        g = gconv_ref[y, :, ln].reshape(strip, SUBL, LANES)
        for a in range(KSIZE):
            e = enc_ref[y + a, :, ln].reshape(wide, SUBL, LANES)
            out = [ge_ref[y + a, j * SUBL : (j + 1) * SUBL, :] for j in range(wide)]
            for b in range(KSIZE):
                o = a * KSIZE + b
                acc_ref[o] += jnp.sum(g * e[b : b + strip], axis=0)
                k = kb_ref[o]
                for j in range(strip):
                    out[j + b] = out[j + b] + g[j] * k
            for j in range(wide):
                ge_ref[y + a, j * SUBL : (j + 1) * SUBL, :] = out[j]
        return c

    lax.fori_loop(0, rows, conv_back, 0)
    xa = xa_ref[...].reshape(high * wmain, chans).astype(BF16)
    ge = ge_ref[...].reshape(high * wmain, LANES).astype(BF16)
    out_ref[...] = jnp.zeros_like(out_ref)
    out_ref[0:chans, :] = tn(xa, ge)
    out_ref[AT_DW : AT_DW + KSIZE * KSIZE, :] = jnp.sum(acc_ref[...], axis=1)
    out_ref[AT_GAIN : AT_GAIN + SUBL, :] = gl_ref[:, ln]
    out_ref[AT_DEC : AT_DEC + dec_ref.shape[0], :] = dec_ref[:, ln]


def vmem(n):
    return [pl.BlockSpec(memory_space=pltpu.VMEM) for _ in range(n)]


def grant(mib):
    return pltpu.CompilerParams(vmem_limit_bytes=mib << 20)


def swapped(value, axis, d):
    size = lax.axis_size(axis)
    return lax.ppermute(value, axis, [(i, i ^ d) for i in range(size)])


def pick_kernel(keep_ref, recv_ref, out_ref):
    out_ref[...] = (keep_ref[...] + recv_ref[...].astype(F32)).astype(out_ref.dtype)


def block_kernel(gate_ref, own_ref, *refs):
    base_ref, out_refs = refs[QUAD - 1], refs[QUAD:]
    total = own_ref[...]
    for ref in refs[: QUAD - 1]:
        total = total + ref[...].astype(F32)
    base_ref[...] = total[0]
    for g in range(1, len(out_refs) + 1):
        out_refs[g - 1][...] = total[g].astype(BF16)


def total_kernel(gate_ref, base_ref, *refs):
    total = base_ref[...]
    for ref in refs[:-1]:
        total = total + ref[...].astype(F32)
    refs[-1][...] = total.astype(BF16)


def hold_kernel(small_ref, *refs):
    out_ref = refs[-1]
    slots, tall, _ = out_ref.shape
    deep = refs[0].shape[1]
    for g in range(slots):
        out_ref[g, :, 0:deep] = refs[g][...]
    high = slots * tall
    for i in range(small_ref.shape[0] // high):
        at = deep + i * LANES
        block = small_ref[i * high : (i + 1) * high, :]
        out_ref[:, :, at : at + LANES] = block.reshape(slots, tall, LANES)


def halve_kernel(a_ref, b_ref, keep_ref, send_ref):
    first = lax.axis_index("sub") == 0
    a, b = a_ref[...], b_ref[...]
    keep_ref[...] = jnp.where(first, a, b)
    send_ref[...] = jnp.where(first, b, a).astype(BF16)


def pair_kernel(mine_ref, other_ref, out_ref):
    out_ref[...] = (mine_ref[...].astype(F32) + other_ref[...].astype(F32)).astype(BF16)


def spread_kernel(*refs):
    mine, other = refs[:QUAD], refs[QUAD : 2 * QUAD]
    up_ref, down_ref, enc_ref, dw_ref, gain_ref, dec_ref, loss_ref = refs[2 * QUAD : -2]
    small_ref, turned_ref = refs[-2:]
    slots, tall, _ = mine[0].shape
    width, hid = up_ref.shape
    chans = enc_ref.shape[0]
    band = lax.axis_index("band")
    sub = lax.axis_index("sub")
    high = slots * tall
    first = sub == 0
    for d in range(QUAD):
        for g in range(slots):
            rows = pl.ds(pl.multiple_of((band ^ reach(d, g)) * tall, tall), tall)
            one = mine[d][g, :, 0:hid].astype(F32)
            two = other[d][g, :, 0:hid].astype(F32)
            up_ref[rows, :] = jnp.where(first, one, two)
            turned_ref[rows, :] = jnp.where(first, two, one)
    for side, core in ((mine, sub), (other, 1 - sub)):
        lanes = pl.ds(pl.multiple_of(core * LANES, LANES), LANES)
        for i in range(SMALL_ROWS // high):
            ln = slice(hid + i * LANES, hid + (i + 1) * LANES)
            a, b, c, e = [side[d][:, :, ln].astype(F32) for d in range(QUAD)]
            small_ref[i * high : (i + 1) * high, lanes] = ((a + b) + (c + e)).reshape(high, LANES)
    for q in range(hid // width):
        ln = slice(q * width, (q + 1) * width)
        down_ref[ln, :] = turned_ref[:, ln].T
    enc_ref[...] = small_ref[0:chans, :]
    dec_ref[...] = small_ref[AT_DEC : AT_DEC + chans, :]
    dw_ref[...] = small_ref[AT_DW : AT_DW + KSIZE * KSIZE, :]
    gain_ref[...] = small_ref[AT_GAIN : AT_GAIN + 1, :]
    loss_ref[...] = jnp.sum(small_ref[AT_LOSS : AT_LOSS + 3, :], axis=(0, 1), keepdims=True)


def local(body, out_shape, mib, name, *args, gates=(), scratch=(), cost=None):
    many = isinstance(out_shape, (list, tuple))
    return pl.pallas_call(
        body,
        out_shape=out_shape,
        in_specs=[pl.BlockSpec(memory_space=pl.ANY) for _ in gates] + vmem(len(args)),
        out_specs=vmem(len(out_shape)) if many else vmem(1)[0],
        scratch_shapes=list(scratch), name=name, compiler_params=grant(mib), cost_estimate=cost,
    )(*gates, *args)


def summed(keep, send, inner, shapes):
    enc, gconv, gr, xa, dw_kernel, gl, dec = inner
    blocks, tall, deep = keep[0].shape
    n = lax.axis_size("band")
    piece = (tall, deep)
    slab = (blocks,) + piece
    high, wmain, _ = xa.shape

    def back(h, gate):
        return local(
            lambda *r: back_kernel(h, *r),
            jax.ShapeDtypeStruct((SMALL_ROWS, LANES), F32), 10, f"back{h}",
            enc, gconv, gr, xa, dw_kernel, gl, dec,
            gates=(gate,),
            scratch=[
                pltpu.VMEM((KSIZE * KSIZE, SUBL, LANES), F32),
                pltpu.VMEM((KSIZE * KSIZE, SUBL, LANES), F32),
                pltpu.VMEM((high, wmain, LANES), F32),
            ],
            cost=pl.CostEstimate(flops=3_000_000_000, bytes_accessed=18_000_000, transcendentals=0),
        )

    got = []
    for d in range(QUAD - 1, -1, -1):
        shape = jax.ShapeDtypeStruct(slab, BF16 if d else F32)
        part = local(pick_kernel, shape, 6, f"pick{d}", keep[d], swapped(send[d], "sub", 1))
        got.append(swapped(part, "band", d) if d else part)
    small_a = back(0, got[-1])
    base, *far = local(
        block_kernel,
        [jax.ShapeDtypeStruct(piece, F32)] + [jax.ShapeDtypeStruct(piece, BF16)] * (blocks - 1),
        8, "block", got[-1], *got[:-1], gates=(small_a,),
    )
    got = [swapped(far[g - 1], "band", QUAD * g) for g in range(1, blocks)]
    small_b = back(1, far[0])
    total = local(
        total_kernel, jax.ShapeDtypeStruct(piece, BF16), 4, "total", base, *got, gates=(small_b,)
    )
    half = (SMALL_ROWS, LANES)
    s_keep, s_send = local(
        halve_kernel,
        [jax.ShapeDtypeStruct(half, F32), jax.ShapeDtypeStruct(half, BF16)],
        4, "halve", small_a, small_b,
    )
    small = local(
        pick_kernel, jax.ShapeDtypeStruct(half, BF16), 4, "chip", s_keep, swapped(s_send, "sub", 1)
    )
    got = [swapped(total, "band", QUAD * g) for g in range(1, blocks)]
    step = QUAD
    while step < n:
        small = local(
            pair_kernel, jax.ShapeDtypeStruct(half, BF16), 4, "pair",
            small, swapped(small, "band", step),
        )
        step *= 2
    hold = local(
        hold_kernel,
        jax.ShapeDtypeStruct((blocks, tall, deep + SMALL_ROWS // (blocks * tall) * LANES), BF16),
        4, "hold", small, total, *got,
    )
    mine = [hold] + [swapped(hold, "band", d) for d in range(1, QUAD)]
    other = [swapped(value, "sub", 1) for value in mine]
    width, hid = shapes[0]
    return local(
        spread_kernel, [jax.ShapeDtypeStruct(s, F32) for s in shapes], 16, "spread",
        *mine, *other,
        scratch=[
            pltpu.VMEM((SMALL_ROWS, width), F32),
            pltpu.VMEM((width, hid), F32),
        ],
    )


def shards(state, target, tile_plan, w_enc, dw_kernel, norm_gain, w_up, w_down, w_dec):
    chans, rows, cols = state.shape
    width = w_enc.shape[1]
    hid = w_up.shape[1]
    main = cols
    wmain = cols + 2 * RIM * SUBL
    high = rows + 2 * RIM
    n_band = lax.axis_size("band")

    st = state.transpose(1, 0, 2)
    tgt = target.transpose(1, 0, 2)
    edges = jnp.concatenate([st[:, :, cols - RIM :], st[:, :, :RIM]], axis=2)
    other = swapped(edges, "sub", 1)
    last = jnp.concatenate([st[rows - RIM :], other[rows - RIM :]], axis=2)
    first = jnp.concatenate([st[:RIM], other[:RIM]], axis=2)
    odd = (lax.axis_index("band") & 1) == 1
    near = lax.ppermute(
        jnp.where(odd, first, last), "band", [(i, i ^ 1) for i in range(n_band)]
    )
    pairs = [(i, i + 1) for i in range(1, n_band - 1, 2)]
    far = lax.ppermute(jnp.where(odd, last, first), "band", pairs + [(j, i) for i, j in pairs])

    cells = rows * main
    chunk = GROUP * main
    n = n_band
    tall = width // n
    slab = (n // QUAD, tall, hid)
    new, *rest = pl.pallas_call(
        step_kernel,
        out_shape=[
            jax.ShapeDtypeStruct((rows, chans, cols), BF16),
            *[jax.ShapeDtypeStruct(slab, F32)] * QUAD,
            *[jax.ShapeDtypeStruct(slab, BF16)] * QUAD,
            jax.ShapeDtypeStruct((high, wmain, width), F32),
            jax.ShapeDtypeStruct((rows, main, width), F32),
            jax.ShapeDtypeStruct((cells, width), BF16),
            jax.ShapeDtypeStruct((high, wmain, chans), F32),
            jax.ShapeDtypeStruct((SUBL, width), F32),
            jax.ShapeDtypeStruct((AT_DW - AT_DEC, width), F32),
        ],
        in_specs=vmem(12), out_specs=vmem(7 + 2 * QUAD),
        scratch_shapes=[
            pltpu.VMEM((KSIZE * KSIZE, SUBL, width), F32),
            pltpu.VMEM((chunk, LANES), F32),
            pltpu.VMEM((cells, hid), BF16),
            pltpu.VMEM((chunk, hid), F32),
            pltpu.VMEM((cells, hid), BF16),
            pltpu.VMEM((chunk, width), F32),
            pltpu.VMEM((cells, width), BF16),
            pltpu.VMEM((chunk, width), F32),
            pltpu.VMEM((n, tall, 2 * hid), F32),
        ],
        name="step",
        compiler_params=grant(36),
    )(
        tile_plan, st, near, far, other, tgt,
        w_enc, dw_kernel, norm_gain.reshape(1, width), w_up, w_down, w_dec.T,
    )
    g_up, g_down, g_enc, g_dw, g_gain, g_dec, loss = summed(
        rest[:QUAD], rest[QUAD : 2 * QUAD],
        (*rest[2 * QUAD : 2 * QUAD + 4], dw_kernel, *rest[2 * QUAD + 4 :]),
        [(width, hid), (hid, width), (chans, width), dw_kernel.shape, (1, width), (chans, width), (1, 1)],
    )
    return (
        new.transpose(1, 0, 2), loss.reshape(1), g_enc, g_dw, g_gain.reshape(width),
        g_up, g_down, g_dec.T,
    )


def solution(mesh):
    return jax.shard_map(
        shards,
        mesh=mesh,
        in_specs=(
            P("groups", "band", "sub"),
            P("groups", "band", "sub"),
            P("groups", None),
            P(),
            P(),
            P(),
            P(),
            P(),
            P(),
        ),
        out_specs=(
            P("groups", "band", "sub"),
            P("groups"),
            P("groups", None),
            P("groups", None),
            P("groups"),
            P("groups", None),
            P("groups", None),
            P("groups", None),
        ),
        check_vma=False,
    )
```

```python
import math

import jax
import jax.numpy as jnp
from jax import lax
from jax.experimental import pallas as pl
from jax.experimental.pallas import tpu as pltpu
from jax.sharding import PartitionSpec as P

F32 = jnp.float32
BF16 = jnp.bfloat16

KSIZE = 7
RIM = KSIZE // 2
PATCH = 12
LANES = 128
SUBL = 8
SMALL_ROWS = 256
GROUP = 12
UNROLL = 4
AT_DEC = 80
AT_DW = 160
AT_GAIN = 216
AT_LOSS = 217
GELU_A = math.sqrt(2.0 / math.pi)
GELU_B = GELU_A * 0.044715


def nn(a, b):
    return lax.dot_general(a, b, (((1,), (0,)), ((), ())), preferred_element_type=F32)


def nt(a, b):
    return lax.dot_general(a, b, (((1,), (1,)), ((), ())), preferred_element_type=F32)


def tn(a, b):
    return lax.dot_general(a, b, (((0,), (0,)), ((), ())), preferred_element_type=F32)


QUAD = 4


def reach(d, g):
    return d + QUAD * g


def strip_column(shape, strip, shift):
    r = lax.broadcasted_iota(jnp.int32, shape, 0)
    return (r & (SUBL - 1)) * strip + (r >> 3) - shift


def encode_rows(y, xa_ref, enc_ref, wenc_ref):
    _, wmain, chans = xa_ref.shape
    xa = xa_ref[pl.ds(y, RIM)].reshape(RIM * wmain, chans).astype(BF16)
    enc = nn(xa, wenc_ref[...]).astype(BF16).astype(F32)
    enc_ref[pl.ds(y, RIM)] = enc.reshape(RIM, wmain, enc.shape[1])


def conv_row(y, enc_ref, kb_ref, out_ref):
    _, main, width = out_ref.shape
    strip = main // SUBL
    wide = strip + 2 * RIM
    for h in range(width // LANES):
        ln = slice(h * LANES, (h + 1) * LANES)
        acc = jnp.zeros((strip, SUBL, LANES), F32)
        for a in range(KSIZE):
            e = enc_ref[y + a, :, ln].reshape(wide, SUBL, LANES)
            for b in range(KSIZE):
                acc = acc + e[b : b + strip] * kb_ref[a * KSIZE + b, :, ln]
        out_ref[y, :, ln] = acc.reshape(main, LANES)


def early_kernel(
    gate_ref, st_ref, e_ref, wenc_ref, dw_ref, enc_ref, xa_ref, nrm_ref, kb_ref
):
    rows, chans, cols = st_ref.shape
    width = wenc_ref.shape[1]
    strip = cols // SUBL
    wmain = (strip + 2 * RIM) * SUBL
    col_w = strip_column((wmain, cols), strip, RIM)
    pick = (col_w == lax.broadcasted_iota(jnp.int32, (wmain, cols), 1)).astype(BF16)
    edge = lax.broadcasted_iota(jnp.int32, (wmain, 2 * RIM), 1)
    edge_col = jnp.where(edge < RIM, edge - RIM, edge - RIM + cols)
    pick_edge = (strip_column((wmain, 2 * RIM), strip, RIM) == edge_col).astype(BF16)
    for o in range(KSIZE * KSIZE):
        kb_ref[o] = jnp.broadcast_to(dw_ref[o : o + 1, :].astype(F32), (SUBL, width))
    for i in range(rows):
        xa_ref[i + RIM] = nt(pick, st_ref[i]) + nt(pick_edge, e_ref[i])

    def encode(i, c):
        encode_rows((i + 1) * RIM, xa_ref, enc_ref, wenc_ref)
        return c

    lax.fori_loop(0, rows // RIM, encode, 0)

    def conv(i, c):
        conv_row(RIM + i, enc_ref, kb_ref, nrm_ref)
        return c

    lax.fori_loop(0, rows - 2 * RIM, conv, 0, unroll=2)


def step_kernel(
    plan_ref, st_ref, near_ref, far_ref, enc_in_ref, xa_in_ref, nrm_in_ref, kb_ref, tgt_ref,
    wenc_ref, gain_ref, wup_ref, wdown_ref, wdec_ref,
    new_ref, *rest,
):
    keep_refs, send_refs = rest[:QUAD], rest[QUAD : 2 * QUAD]
    enc_ref, nrm_ref, gr_ref, xa_ref, gl_ref, dec_ref = rest[2 * QUAD : 2 * QUAD + 6]
    istd_ref, act_ref, dg_ref, gp_ref, gs_ref, sc_ref, rs_ref, all_ref = rest[
        2 * QUAD + 6 :
    ]
    rows, chans, cols = st_ref.shape
    width = wenc_ref.shape[1]
    hid = wup_ref.shape[1]
    strip = cols // SUBL
    wide = strip + 2 * RIM
    main = strip * SUBL
    wmain = wide * SUBL
    band = lax.axis_index("band")
    sub = lax.axis_index("sub")
    tiles = cols // PATCH

    full = lax.broadcasted_iota(jnp.int32, (wmain, cols + 2 * RIM), 1)
    left = full - cols - RIM
    full_col = jnp.where(full < cols, full, jnp.where(left < 0, left, left + cols))
    pick_full = (strip_column(full.shape, strip, RIM) == full_col).astype(BF16)
    col_c = strip_column((main, cols), strip, 0)
    place = (col_c == lax.broadcasted_iota(jnp.int32, (main, cols), 1)).astype(BF16)

    wet_all = (plan_ref[...] >= 0).astype(F32)
    inv = 1.0 / (jnp.sum(wet_all, axis=(0, 1), keepdims=True) * float(chans * rows * PATCH))
    wet_row = (plan_ref[pl.ds(band, 1), :] >= 0).astype(F32)
    n_cols = wet_row.shape[1]
    at = lax.broadcasted_iota(jnp.int32, (main, n_cols), 1) - sub * tiles
    cc = strip_column((main, n_cols), strip, 0)
    in_tile = (cc >= at * PATCH) & (cc < at * PATCH + PATCH)
    wet_rows = jnp.sum(jnp.where(in_tile, wet_row, 0.0), axis=1, keepdims=True)
    at_x = lax.broadcasted_iota(jnp.int32, (n_cols, cols), 0) - sub * tiles
    x_x = lax.broadcasted_iota(jnp.int32, (n_cols, cols), 1)
    in_x = ((x_x >= at_x * PATCH) & (x_x < at_x * PATCH + PATCH)).astype(BF16)
    wet_x = nn(jnp.broadcast_to(wet_row, (SUBL, n_cols)).astype(BF16), in_x)[0:1]

    odd = (band & 1) == 1
    for i in range(RIM):
        xa_ref[i] = nt(pick_full, jnp.where(odd, near_ref[i], far_ref[i]))
        xa_ref[i + RIM + rows] = nt(pick_full, jnp.where(odd, far_ref[i], near_ref[i]))
    encode_rows(0, xa_ref, enc_ref, wenc_ref)
    encode_rows(RIM + rows, xa_ref, enc_ref, wenc_ref)
    xa_ref[RIM : RIM + rows] = xa_in_ref[RIM : RIM + rows]
    enc_ref[RIM : RIM + rows] = enc_in_ref[RIM : RIM + rows]
    nrm_ref[RIM : rows - RIM] = nrm_in_ref[RIM : rows - RIM]

    def conv(i, c):
        conv_row(i, enc_ref, kb_ref, nrm_ref)
        conv_row(i + rows - RIM, enc_ref, kb_ref, nrm_ref)
        return c

    lax.fori_loop(0, RIM, conv, 0)

    dec_ref[...] = jnp.zeros_like(dec_ref)
    gl_ref[...] = jnp.zeros_like(gl_ref)
    gain = gain_ref[...]
    group = GROUP
    chunk = group * main
    blocks = hid // width
    wetg = jnp.concatenate([wet_rows] * group, axis=0)

    def mlp(k, loss):
        y0 = k * group
        r0 = pl.multiple_of(k * chunk, chunk)
        v = nrm_ref[pl.ds(y0, group)].reshape(chunk, width)
        cen = v - jnp.mean(v, axis=-1, keepdims=True)
        istd = lax.rsqrt(jnp.mean(cen * cen, axis=-1, keepdims=True) + 1e-06)
        nrm = cen * istd
        nrm_ref[pl.ds(y0, group)] = nrm.reshape(group, main, width)
        istd_ref[...] = jnp.broadcast_to(istd, (chunk, LANES))
        sc_ref[pl.ds(r0, chunk), :] = (nrm * gain).astype(BF16)
        centre = enc_ref[pl.ds(y0 + RIM, group), RIM * SUBL : RIM * SUBL + main, :]
        rs_ref[...] = centre.reshape(chunk, width)

        def up(n, c):
            n0 = pl.multiple_of(n * width, width)
            v = nn(sc_ref[pl.ds(r0, chunk), :], wup_ref[:, pl.ds(n0, width)])
            vv = v * v
            t = jnp.tanh(v * (GELU_A + GELU_B * vv))
            q = 1.0 + t
            soft = 0.5 * v * q
            dg_ref[:, pl.ds(n0, width)] = 0.5 * q + soft * (1.0 - t) * (GELU_A + 3.0 * GELU_B * vv)
            act = soft.astype(BF16)
            act_ref[pl.ds(r0, chunk), pl.ds(n0, width)] = act
            rs_ref[...] += nn(act, wdown_ref[pl.ds(n0, width), :])
            return c

        lax.fori_loop(0, blocks, up, 0, unroll=UNROLL)
        residual = rs_ref[...].astype(BF16)
        base = xa_ref[pl.ds(y0 + RIM, group), RIM * SUBL : RIM * SUBL + main, :]
        pred = base.reshape(chunk, chans) + nt(residual, wdec_ref[...])
        goal = jnp.concatenate([nt(place, tgt_ref[y0 + i]) for i in range(group)], axis=0)
        mis = (pred - goal) * wetg
        for i in range(group):
            back = tn(pred[i * main : (i + 1) * main].astype(BF16), place)
            new_ref[y0 + i] = jnp.where(wet_x > 0.5, back.astype(BF16), st_ref[y0 + i])
        loss = loss + jnp.sum(mis * mis, axis=(0, 1), keepdims=True)
        gout = (mis * (2.0 * inv)).astype(BF16)
        dec_ref[0:chans, :] += tn(gout, residual)
        gres = nn(gout, wdec_ref[...]).astype(BF16)
        gr_ref[pl.ds(r0, chunk), :] = gres
        gs_ref[...] = jnp.zeros_like(gs_ref)

        def down(n, c):
            n0 = pl.multiple_of(n * width, width)
            ga = nt(gr_ref[pl.ds(r0, chunk), :], wdown_ref[pl.ds(n0, width), :])
            gp = (ga * dg_ref[:, pl.ds(n0, width)]).astype(BF16)
            gp_ref[pl.ds(r0, chunk), pl.ds(n0, width)] = gp
            gs_ref[...] += nt(gp, wup_ref[:, pl.ds(n0, width)])
            return c

        lax.fori_loop(0, blocks, down, 0, unroll=UNROLL)
        gs = gs_ref[...]
        nrm = nrm_ref[pl.ds(y0, group)].reshape(chunk, width)
        prod = gs * nrm
        gl_ref[0:1, :] += jnp.sum(prod, axis=0, keepdims=True)
        g = gs * gain
        m1 = jnp.mean(g, axis=-1, keepdims=True)
        m2 = jnp.mean(g * nrm, axis=-1, keepdims=True)
        gc = g - m1 - nrm * m2
        istd = istd_ref[...]
        for h in range(width // LANES):
            ln = slice(h * LANES, (h + 1) * LANES)
            nrm_ref[pl.ds(y0, group), :, ln] = (gc[:, ln] * istd).reshape(group, main, LANES)
        return loss

    loss = lax.fori_loop(0, rows // group, mlp, jnp.zeros((1, 1), F32))
    lane = lax.broadcasted_iota(jnp.int32, (1, width), 1)
    rest = jnp.where(lane == band * lax.axis_size("sub") + sub, loss * inv, 0.0)
    for i in range(3):
        term = rest.astype(BF16).astype(F32)
        gl_ref[1 + i : 2 + i, :] = term
        rest = rest - term

    n_piece, tall, _ = all_ref.shape

    def wgrad(n, c):
        n0 = pl.multiple_of(n * width, width)
        g_up = tn(sc_ref[...], gp_ref[:, pl.ds(n0, width)])
        g_down = tn(gr_ref[...], act_ref[:, pl.ds(n0, width)])
        all_ref[:, :, pl.ds(n0, width)] = g_up.reshape(n_piece, tall, width)
        all_ref[:, :, pl.ds(pl.multiple_of(hid + n0, width), width)] = g_down.reshape(
            n_piece, tall, width
        )
        return c

    lax.fori_loop(0, blocks, wgrad, 0, unroll=UNROLL)

    mine = pl.ds(pl.multiple_of(sub * hid, hid), hid)
    theirs = pl.ds(pl.multiple_of((1 - sub) * hid, hid), hid)
    for d in range(QUAD):
        for g in range(n_piece // QUAD):
            keep_refs[d][g] = all_ref[band ^ reach(d, g), :, mine]
            send_refs[d][g] = all_ref[band ^ reach(d, g), :, theirs].astype(BF16)


def back_kernel(
    h, gate_ref, enc_ref, gconv_ref, gr_ref, xa_ref, dw_ref, gl_ref, dec_ref,
    out_ref, kb_ref, acc_ref, ge_ref,
):
    rows, main, _ = gconv_ref.shape
    high, wmain, chans = xa_ref.shape
    strip = main // SUBL
    wide = wmain // SUBL
    ln = slice(h * LANES, (h + 1) * LANES)
    for o in range(KSIZE * KSIZE):
        kb_ref[o] = jnp.broadcast_to(dw_ref[o : o + 1, ln].astype(F32), (SUBL, LANES))
    acc_ref[...] = jnp.zeros_like(acc_ref)
    ge_ref[...] = jnp.zeros_like(ge_ref)
    centre = gr_ref[:, ln].astype(F32).reshape(rows, main, LANES)
    ge_ref[RIM : RIM + rows, RIM * SUBL : RIM * SUBL + main, :] = centre

    def conv_back(y, c):
        g = gconv_ref[y, :, ln].reshape(strip, SUBL, LANES)
        for a in range(KSIZE):
            e = enc_ref[y + a, :, ln].reshape(wide, SUBL, LANES)
            out = [ge_ref[y + a, j * SUBL : (j + 1) * SUBL, :] for j in range(wide)]
            for b in range(KSIZE):
                o = a * KSIZE + b
                acc_ref[o] += jnp.sum(g * e[b : b + strip], axis=0)
                k = kb_ref[o]
                for j in range(strip):
                    out[j + b] = out[j + b] + g[j] * k
            for j in range(wide):
                ge_ref[y + a, j * SUBL : (j + 1) * SUBL, :] = out[j]
        return c

    lax.fori_loop(0, rows, conv_back, 0)
    xa = xa_ref[...].reshape(high * wmain, chans).astype(BF16)
    ge = ge_ref[...].reshape(high * wmain, LANES).astype(BF16)
    out_ref[...] = jnp.zeros_like(out_ref)
    out_ref[0:chans, :] = tn(xa, ge)
    out_ref[AT_DW : AT_DW + KSIZE * KSIZE, :] = jnp.sum(acc_ref[...], axis=1)
    out_ref[AT_GAIN : AT_GAIN + SUBL, :] = gl_ref[:, ln]
    out_ref[AT_DEC : AT_DEC + dec_ref.shape[0], :] = dec_ref[:, ln]


def vmem(n):
    return [pl.BlockSpec(memory_space=pltpu.VMEM) for _ in range(n)]


def grant(mib):
    return pltpu.CompilerParams(vmem_limit_bytes=mib << 20)


def swapped(value, axis, d):
    size = lax.axis_size(axis)
    return lax.ppermute(value, axis, [(i, i ^ d) for i in range(size)])


def pick_kernel(keep_ref, recv_ref, out_ref):
    out_ref[...] = (keep_ref[...] + recv_ref[...].astype(F32)).astype(out_ref.dtype)


def block_kernel(gate_ref, own_ref, *refs):
    base_ref, out_refs = refs[QUAD - 1], refs[QUAD:]
    total = own_ref[...]
    for ref in refs[: QUAD - 1]:
        total = total + ref[...].astype(F32)
    base_ref[...] = total[0]
    for g in range(1, len(out_refs) + 1):
        out_refs[g - 1][...] = total[g].astype(BF16)


def total_kernel(gate_ref, base_ref, *refs):
    total = base_ref[...]
    for ref in refs[:-1]:
        total = total + ref[...].astype(F32)
    refs[-1][...] = total.astype(BF16)


def hold_kernel(small_ref, *refs):
    out_ref = refs[-1]
    slots, tall, _ = out_ref.shape
    deep = refs[0].shape[1]
    for g in range(slots):
        out_ref[g, :, 0:deep] = refs[g][...]
    high = slots * tall
    for i in range(small_ref.shape[0] // high):
        at = deep + i * LANES
        block = small_ref[i * high : (i + 1) * high, :]
        out_ref[:, :, at : at + LANES] = block.reshape(slots, tall, LANES)


def halve_kernel(a_ref, b_ref, keep_ref, send_ref):
    first = lax.axis_index("sub") == 0
    a, b = a_ref[...], b_ref[...]
    keep_ref[...] = jnp.where(first, a, b)
    send_ref[...] = jnp.where(first, b, a).astype(BF16)


def pair_kernel(mine_ref, other_ref, out_ref):
    out_ref[...] = (mine_ref[...].astype(F32) + other_ref[...].astype(F32)).astype(BF16)


def spread_kernel(*refs):
    mine, other = refs[:QUAD], refs[QUAD : 2 * QUAD]
    up_ref, down_ref, enc_ref, dw_ref, gain_ref, dec_ref, loss_ref = refs[2 * QUAD : -2]
    small_ref, turned_ref = refs[-2:]
    slots, tall, _ = mine[0].shape
    width, hid = up_ref.shape
    chans = enc_ref.shape[0]
    band = lax.axis_index("band")
    sub = lax.axis_index("sub")
    high = slots * tall
    first = sub == 0
    for d in range(QUAD):
        for g in range(slots):
            rows = pl.ds(pl.multiple_of((band ^ reach(d, g)) * tall, tall), tall)
            one = mine[d][g, :, 0:hid].astype(F32)
            two = other[d][g, :, 0:hid].astype(F32)
            up_ref[rows, :] = jnp.where(first, one, two)
            turned_ref[rows, :] = jnp.where(first, two, one)
    for side, core in ((mine, sub), (other, 1 - sub)):
        lanes = pl.ds(pl.multiple_of(core * LANES, LANES), LANES)
        for i in range(SMALL_ROWS // high):
            ln = slice(hid + i * LANES, hid + (i + 1) * LANES)
            a, b, c, e = [side[d][:, :, ln].astype(F32) for d in range(QUAD)]
            small_ref[i * high : (i + 1) * high, lanes] = ((a + b) + (c + e)).reshape(high, LANES)
    for q in range(hid // width):
        ln = slice(q * width, (q + 1) * width)
        down_ref[ln, :] = turned_ref[:, ln].T
    enc_ref[...] = small_ref[0:chans, :]
    dec_ref[...] = small_ref[AT_DEC : AT_DEC + chans, :]
    dw_ref[...] = small_ref[AT_DW : AT_DW + KSIZE * KSIZE, :]
    gain_ref[...] = small_ref[AT_GAIN : AT_GAIN + 1, :]
    loss_ref[...] = jnp.sum(small_ref[AT_LOSS : AT_LOSS + 3, :], axis=(0, 1), keepdims=True)


def local(body, out_shape, mib, name, *args, gates=(), scratch=(), cost=None):
    many = isinstance(out_shape, (list, tuple))
    return pl.pallas_call(
        body,
        out_shape=out_shape,
        in_specs=[pl.BlockSpec(memory_space=pl.ANY) for _ in gates] + vmem(len(args)),
        out_specs=vmem(len(out_shape)) if many else vmem(1)[0],
        scratch_shapes=list(scratch), name=name, compiler_params=grant(mib), cost_estimate=cost,
    )(*gates, *args)


def summed(keep, send, inner, shapes):
    enc, gconv, gr, xa, dw_kernel, gl, dec = inner
    blocks, tall, deep = keep[0].shape
    n = lax.axis_size("band")
    piece = (tall, deep)
    slab = (blocks,) + piece
    high, wmain, _ = xa.shape

    def back(h, gate):
        return local(
            lambda *r: back_kernel(h, *r),
            jax.ShapeDtypeStruct((SMALL_ROWS, LANES), F32), 10, f"back{h}",
            enc, gconv, gr, xa, dw_kernel, gl, dec,
            gates=(gate,),
            scratch=[
                pltpu.VMEM((KSIZE * KSIZE, SUBL, LANES), F32),
                pltpu.VMEM((KSIZE * KSIZE, SUBL, LANES), F32),
                pltpu.VMEM((high, wmain, LANES), F32),
            ],
            cost=pl.CostEstimate(flops=3_000_000_000, bytes_accessed=18_000_000, transcendentals=0),
        )

    got = []
    for d in range(QUAD - 1, -1, -1):
        shape = jax.ShapeDtypeStruct(slab, BF16 if d else F32)
        part = local(pick_kernel, shape, 6, f"pick{d}", keep[d], swapped(send[d], "sub", 1))
        got.append(swapped(part, "band", d) if d else part)
    small_a = back(0, got[-1])
    base, *far = local(
        block_kernel,
        [jax.ShapeDtypeStruct(piece, F32)] + [jax.ShapeDtypeStruct(piece, BF16)] * (blocks - 1),
        8, "block", got[-1], *got[:-1], gates=(small_a,),
    )
    got = [swapped(far[g - 1], "band", QUAD * g) for g in range(1, blocks)]
    small_b = back(1, far[0])
    total = local(
        total_kernel, jax.ShapeDtypeStruct(piece, BF16), 4, "total", base, *got, gates=(small_b,)
    )
    half = (SMALL_ROWS, LANES)
    s_keep, s_send = local(
        halve_kernel,
        [jax.ShapeDtypeStruct(half, F32), jax.ShapeDtypeStruct(half, BF16)],
        4, "halve", small_a, small_b,
    )
    small = local(
        pick_kernel, jax.ShapeDtypeStruct(half, BF16), 4, "chip", s_keep, swapped(s_send, "sub", 1)
    )
    got = [swapped(total, "band", QUAD * g) for g in range(1, blocks)]
    step = QUAD
    while step < n:
        small = local(
            pair_kernel, jax.ShapeDtypeStruct(half, BF16), 4, "pair",
            small, swapped(small, "band", step),
        )
        step *= 2
    hold = local(
        hold_kernel,
        jax.ShapeDtypeStruct((blocks, tall, deep + SMALL_ROWS // (blocks * tall) * LANES), BF16),
        4, "hold", small, total, *got,
    )
    mine = [hold] + [swapped(hold, "band", d) for d in range(1, QUAD)]
    other = [swapped(value, "sub", 1) for value in mine]
    width, hid = shapes[0]
    return local(
        spread_kernel, [jax.ShapeDtypeStruct(s, F32) for s in shapes], 16, "spread",
        *mine, *other,
        scratch=[
            pltpu.VMEM((SMALL_ROWS, width), F32),
            pltpu.VMEM((width, hid), F32),
        ],
    )


def shards(state, target, tile_plan, w_enc, dw_kernel, norm_gain, w_up, w_down, w_dec):
    chans, rows, cols = state.shape
    width = w_enc.shape[1]
    hid = w_up.shape[1]
    main = cols
    wmain = cols + 2 * RIM * SUBL
    high = rows + 2 * RIM
    n_band = lax.axis_size("band")

    st = state.transpose(1, 0, 2)
    tgt = target.transpose(1, 0, 2)
    edges = jnp.concatenate([st[:, :, cols - RIM :], st[:, :, :RIM]], axis=2)
    other = swapped(edges, "sub", 1)
    last = jnp.concatenate([st[rows - RIM :], other[rows - RIM :]], axis=2)
    first = jnp.concatenate([st[:RIM], other[:RIM]], axis=2)
    odd = (lax.axis_index("band") & 1) == 1
    near = lax.ppermute(
        jnp.where(odd, first, last), "band", [(i, i ^ 1) for i in range(n_band)]
    )
    pairs = [(i, i + 1) for i in range(1, n_band - 1, 2)]
    to_far = jnp.where(odd, last, first)
    far = lax.ppermute(to_far, "band", pairs + [(j, i) for i, j in pairs])

    cells = rows * main
    chunk = GROUP * main
    n = n_band
    tall = width // n
    slab = (n // QUAD, tall, hid)
    enc, xa, nrm, kb = local(
        early_kernel,
        [
            jax.ShapeDtypeStruct((high, wmain, width), F32),
            jax.ShapeDtypeStruct((high, wmain, chans), F32),
            jax.ShapeDtypeStruct((rows, main, width), F32),
            jax.ShapeDtypeStruct((KSIZE * KSIZE, SUBL, width), F32),
        ],
        12, "early", st, other, w_enc, dw_kernel, gates=(to_far,),
        cost=pl.CostEstimate(flops=3_000_000_000, bytes_accessed=15_000_000, transcendentals=0),
    )
    new, *rest = pl.pallas_call(
        step_kernel,
        out_shape=[
            jax.ShapeDtypeStruct((rows, chans, cols), BF16),
            *[jax.ShapeDtypeStruct(slab, F32)] * QUAD,
            *[jax.ShapeDtypeStruct(slab, BF16)] * QUAD,
            jax.ShapeDtypeStruct((high, wmain, width), F32),
            jax.ShapeDtypeStruct((rows, main, width), F32),
            jax.ShapeDtypeStruct((cells, width), BF16),
            jax.ShapeDtypeStruct((high, wmain, chans), F32),
            jax.ShapeDtypeStruct((SUBL, width), F32),
            jax.ShapeDtypeStruct((AT_DW - AT_DEC, width), F32),
        ],
        in_specs=vmem(14), out_specs=vmem(7 + 2 * QUAD),
        scratch_shapes=[
            pltpu.VMEM((chunk, LANES), F32),
            pltpu.VMEM((cells, hid), BF16),
            pltpu.VMEM((chunk, hid), F32),
            pltpu.VMEM((cells, hid), BF16),
            pltpu.VMEM((chunk, width), F32),
            pltpu.VMEM((cells, width), BF16),
            pltpu.VMEM((chunk, width), F32),
            pltpu.VMEM((n, tall, 2 * hid), F32),
        ],
        name="step",
        compiler_params=grant(36),
    )(
        tile_plan, st, near, far, enc, xa, nrm, kb, tgt,
        w_enc, norm_gain.reshape(1, width), w_up, w_down, w_dec.T,
    )
    g_up, g_down, g_enc, g_dw, g_gain, g_dec, loss = summed(
        rest[:QUAD], rest[QUAD : 2 * QUAD],
        (*rest[2 * QUAD : 2 * QUAD + 4], dw_kernel, *rest[2 * QUAD + 4 :]),
        [(width, hid), (hid, width), (chans, width), dw_kernel.shape, (1, width), (chans, width), (1, 1)],
    )
    return (
        new.transpose(1, 0, 2), loss.reshape(1), g_enc, g_dw, g_gain.reshape(width),
        g_up, g_down, g_dec.T,
    )


def solution(mesh):
    return jax.shard_map(
        shards,
        mesh=mesh,
        in_specs=(
            P("groups", "band", "sub"),
            P("groups", "band", "sub"),
            P("groups", None),
            P(),
            P(),
            P(),
            P(),
            P(),
            P(),
        ),
        out_specs=(
            P("groups", "band", "sub"),
            P("groups"),
            P("groups", None),
            P("groups", None),
            P("groups"),
            P("groups", None),
            P("groups", None),
            P("groups", None),
        ),
        check_vma=False,
    )
```

```python
import math

import jax
import jax.numpy as jnp
from jax import lax
from jax.experimental import pallas as pl
from jax.experimental.pallas import tpu as pltpu
from jax.sharding import PartitionSpec as P

F32 = jnp.float32
BF16 = jnp.bfloat16

KSIZE = 7
RIM = KSIZE // 2
PATCH = 12
LANES = 128
SUBL = 8
SMALL_ROWS = 256
GROUP = 12
UNROLL = 4
AT_DEC = 80
AT_DW = 160
AT_GAIN = 216
AT_LOSS = 217
GELU_A = math.sqrt(2.0 / math.pi)
GELU_B = GELU_A * 0.044715


def nn(a, b):
    return lax.dot_general(a, b, (((1,), (0,)), ((), ())), preferred_element_type=F32)


def nt(a, b):
    return lax.dot_general(a, b, (((1,), (1,)), ((), ())), preferred_element_type=F32)


def tn(a, b):
    return lax.dot_general(a, b, (((0,), (0,)), ((), ())), preferred_element_type=F32)


QUAD = 4


def reach(d, g):
    return d + QUAD * g


def strip_column(shape, strip, shift):
    r = lax.broadcasted_iota(jnp.int32, shape, 0)
    return (r & (SUBL - 1)) * strip + (r >> 3) - shift


def encode_rows(y, xa_ref, enc_ref, wenc_ref):
    _, wmain, chans = xa_ref.shape
    xa = xa_ref[pl.ds(y, RIM)].reshape(RIM * wmain, chans).astype(BF16)
    enc = nn(xa, wenc_ref[...]).astype(BF16).astype(F32)
    enc_ref[pl.ds(y, RIM)] = enc.reshape(RIM, wmain, enc.shape[1])


def conv_row(y, enc_ref, kb_ref, out_ref):
    _, main, width = out_ref.shape
    strip = main // SUBL
    wide = strip + 2 * RIM
    for h in range(width // LANES):
        ln = slice(h * LANES, (h + 1) * LANES)
        acc = jnp.zeros((strip, SUBL, LANES), F32)
        for a in range(KSIZE):
            e = enc_ref[y + a, :, ln].reshape(wide, SUBL, LANES)
            for b in range(KSIZE):
                acc = acc + e[b : b + strip] * kb_ref[a * KSIZE + b, :, ln]
        out_ref[y, :, ln] = acc.reshape(main, LANES)


def early_kernel(
    gate_ref, st_ref, e_ref, wenc_ref, dw_ref, enc_ref, xa_ref, nrm_ref, kb_ref
):
    rows, chans, cols = st_ref.shape
    width = wenc_ref.shape[1]
    strip = cols // SUBL
    wmain = (strip + 2 * RIM) * SUBL
    col_w = strip_column((wmain, cols), strip, RIM)
    pick = (col_w == lax.broadcasted_iota(jnp.int32, (wmain, cols), 1)).astype(BF16)
    edge = lax.broadcasted_iota(jnp.int32, (wmain, 2 * RIM), 1)
    edge_col = jnp.where(edge < RIM, edge - RIM, edge - RIM + cols)
    pick_edge = (strip_column((wmain, 2 * RIM), strip, RIM) == edge_col).astype(BF16)
    for o in range(KSIZE * KSIZE):
        kb_ref[o] = jnp.broadcast_to(dw_ref[o : o + 1, :].astype(F32), (SUBL, width))
    for i in range(rows):
        xa_ref[i + RIM] = nt(pick, st_ref[i]) + nt(pick_edge, e_ref[i])

    def encode(i, c):
        encode_rows((i + 1) * RIM, xa_ref, enc_ref, wenc_ref)
        return c

    lax.fori_loop(0, rows // RIM, encode, 0)

    def conv(i, c):
        conv_row(RIM + i, enc_ref, kb_ref, nrm_ref)
        return c

    lax.fori_loop(0, rows - 2 * RIM, conv, 0, unroll=2)


def step_kernel(
    plan_ref, st_ref, near_ref, far_ref, enc_in_ref, xa_in_ref, nrm_in_ref, kb_ref, tgt_ref,
    wenc_ref, gain_ref, wup_ref, wdown_ref, wdec_ref,
    new_ref, *rest,
):
    keep_refs, send_refs = rest[:QUAD], rest[QUAD : 2 * QUAD]
    enc_ref, nrm_ref, gr_ref, xa_ref, gl_ref, dec_ref = rest[2 * QUAD : 2 * QUAD + 6]
    istd_ref, act_ref, dg_ref, gp_ref, gs_ref, sc_ref, rs_ref, all_ref = rest[
        2 * QUAD + 6 :
    ]
    rows, chans, cols = st_ref.shape
    width = wenc_ref.shape[1]
    hid = wup_ref.shape[1]
    strip = cols // SUBL
    wide = strip + 2 * RIM
    main = strip * SUBL
    wmain = wide * SUBL
    band = lax.axis_index("band")
    sub = lax.axis_index("sub")
    tiles = cols // PATCH

    full = lax.broadcasted_iota(jnp.int32, (wmain, cols + 2 * RIM), 1)
    left = full - cols - RIM
    full_col = jnp.where(full < cols, full, jnp.where(left < 0, left, left + cols))
    pick_full = (strip_column(full.shape, strip, RIM) == full_col).astype(BF16)
    col_c = strip_column((main, cols), strip, 0)
    place = (col_c == lax.broadcasted_iota(jnp.int32, (main, cols), 1)).astype(BF16)

    wet_all = (plan_ref[...] >= 0).astype(F32)
    inv = 1.0 / (jnp.sum(wet_all, axis=(0, 1), keepdims=True) * float(chans * rows * PATCH))
    wet_row = (plan_ref[pl.ds(band, 1), :] >= 0).astype(F32)
    n_cols = wet_row.shape[1]
    at = lax.broadcasted_iota(jnp.int32, (main, n_cols), 1) - sub * tiles
    cc = strip_column((main, n_cols), strip, 0)
    in_tile = (cc >= at * PATCH) & (cc < at * PATCH + PATCH)
    wet_rows = jnp.sum(jnp.where(in_tile, wet_row, 0.0), axis=1, keepdims=True)
    at_x = lax.broadcasted_iota(jnp.int32, (n_cols, cols), 0) - sub * tiles
    x_x = lax.broadcasted_iota(jnp.int32, (n_cols, cols), 1)
    in_x = ((x_x >= at_x * PATCH) & (x_x < at_x * PATCH + PATCH)).astype(BF16)
    wet_x = nn(jnp.broadcast_to(wet_row, (SUBL, n_cols)).astype(BF16), in_x)[0:1]

    odd = (band & 1) == 1
    for i in range(RIM):
        xa_ref[i] = nt(pick_full, jnp.where(odd, near_ref[i], far_ref[i]))
        xa_ref[i + RIM + rows] = nt(pick_full, jnp.where(odd, far_ref[i], near_ref[i]))
    encode_rows(0, xa_ref, enc_ref, wenc_ref)
    encode_rows(RIM + rows, xa_ref, enc_ref, wenc_ref)
    xa_ref[RIM : RIM + rows] = xa_in_ref[RIM : RIM + rows]
    enc_ref[RIM : RIM + rows] = enc_in_ref[RIM : RIM + rows]
    nrm_ref[RIM : rows - RIM] = nrm_in_ref[RIM : rows - RIM]

    def conv(i, c):
        conv_row(i, enc_ref, kb_ref, nrm_ref)
        conv_row(i + rows - RIM, enc_ref, kb_ref, nrm_ref)
        return c

    lax.fori_loop(0, RIM, conv, 0)

    dec_ref[...] = jnp.zeros_like(dec_ref)
    gl_ref[...] = jnp.zeros_like(gl_ref)
    gain = gain_ref[...]
    group = GROUP
    chunk = group * main
    blocks = hid // width
    wetg = jnp.concatenate([wet_rows] * group, axis=0)

    def mlp(k, loss):
        y0 = k * group
        r0 = pl.multiple_of(k * chunk, chunk)
        v = nrm_ref[pl.ds(y0, group)].reshape(chunk, width)
        cen = v - jnp.mean(v, axis=-1, keepdims=True)
        istd = lax.rsqrt(jnp.mean(cen * cen, axis=-1, keepdims=True) + 1e-06)
        nrm = cen * istd
        nrm_ref[pl.ds(y0, group)] = nrm.reshape(group, main, width)
        istd_ref[...] = jnp.broadcast_to(istd, (chunk, LANES))
        sc_ref[pl.ds(r0, chunk), :] = (nrm * gain).astype(BF16)
        centre = enc_ref[pl.ds(y0 + RIM, group), RIM * SUBL : RIM * SUBL + main, :]
        rs_ref[...] = centre.reshape(chunk, width)

        def up(n, c):
            n0 = pl.multiple_of(n * width, width)
            v = nn(sc_ref[pl.ds(r0, chunk), :], wup_ref[:, pl.ds(n0, width)])
            vv = v * v
            t = jnp.tanh(v * (GELU_A + GELU_B * vv))
            q = 1.0 + t
            soft = 0.5 * v * q
            dg_ref[:, pl.ds(n0, width)] = 0.5 * q + soft * (1.0 - t) * (GELU_A + 3.0 * GELU_B * vv)
            act = soft.astype(BF16)
            act_ref[pl.ds(r0, chunk), pl.ds(n0, width)] = act
            rs_ref[...] += nn(act, wdown_ref[pl.ds(n0, width), :])
            return c

        lax.fori_loop(0, blocks, up, 0, unroll=UNROLL)
        residual = rs_ref[...].astype(BF16)
        base = xa_ref[pl.ds(y0 + RIM, group), RIM * SUBL : RIM * SUBL + main, :]
        pred = base.reshape(chunk, chans) + nt(residual, wdec_ref[...])
        goal = jnp.concatenate([nt(place, tgt_ref[y0 + i]) for i in range(group)], axis=0)
        mis = (pred - goal) * wetg
        for i in range(group):
            back = tn(pred[i * main : (i + 1) * main].astype(BF16), place)
            new_ref[y0 + i] = jnp.where(wet_x > 0.5, back.astype(BF16), st_ref[y0 + i])
        loss = loss + jnp.sum(mis * mis, axis=(0, 1), keepdims=True)
        gout = (mis * (2.0 * inv)).astype(BF16)
        dec_ref[0:chans, :] += tn(gout, residual)
        gres = nn(gout, wdec_ref[...]).astype(BF16)
        gr_ref[pl.ds(r0, chunk), :] = gres
        gs_ref[...] = jnp.zeros_like(gs_ref)

        def down(n, c):
            n0 = pl.multiple_of(n * width, width)
            ga = nt(gr_ref[pl.ds(r0, chunk), :], wdown_ref[pl.ds(n0, width), :])
            gp = (ga * dg_ref[:, pl.ds(n0, width)]).astype(BF16)
            gp_ref[pl.ds(r0, chunk), pl.ds(n0, width)] = gp
            gs_ref[...] += nt(gp, wup_ref[:, pl.ds(n0, width)])
            return c

        lax.fori_loop(0, blocks, down, 0, unroll=UNROLL)
        gs = gs_ref[...]
        nrm = nrm_ref[pl.ds(y0, group)].reshape(chunk, width)
        prod = gs * nrm
        gl_ref[0:1, :] += jnp.sum(prod, axis=0, keepdims=True)
        g = gs * gain
        m1 = jnp.mean(g, axis=-1, keepdims=True)
        m2 = jnp.mean(g * nrm, axis=-1, keepdims=True)
        gc = g - m1 - nrm * m2
        istd = istd_ref[...]
        for h in range(width // LANES):
            ln = slice(h * LANES, (h + 1) * LANES)
            nrm_ref[pl.ds(y0, group), :, ln] = (gc[:, ln] * istd).reshape(group, main, LANES)
        return loss

    loss = lax.fori_loop(0, rows // group, mlp, jnp.zeros((1, 1), F32))
    lane = lax.broadcasted_iota(jnp.int32, (1, width), 1)
    rest = jnp.where(lane == band * lax.axis_size("sub") + sub, loss * inv, 0.0)
    for i in range(3):
        term = rest.astype(BF16).astype(F32)
        gl_ref[1 + i : 2 + i, :] = term
        rest = rest - term

    n_piece, tall, _ = all_ref.shape

    def wgrad(n, c):
        n0 = pl.multiple_of(n * width, width)
        g_up = tn(sc_ref[...], gp_ref[:, pl.ds(n0, width)])
        g_down = tn(gr_ref[...], act_ref[:, pl.ds(n0, width)])
        all_ref[:, :, pl.ds(n0, width)] = g_up.reshape(n_piece, tall, width)
        all_ref[:, :, pl.ds(pl.multiple_of(hid + n0, width), width)] = g_down.reshape(
            n_piece, tall, width
        )
        return c

    lax.fori_loop(0, blocks, wgrad, 0, unroll=UNROLL)

    mine = pl.ds(pl.multiple_of(sub * hid, hid), hid)
    theirs = pl.ds(pl.multiple_of((1 - sub) * hid, hid), hid)
    for d in range(QUAD):
        for g in range(n_piece // QUAD):
            keep_refs[d][g] = all_ref[band ^ reach(d, g), :, mine]
            send_refs[d][g] = all_ref[band ^ reach(d, g), :, theirs].astype(BF16)


def back_kernel(
    h, gate_ref, enc_ref, gconv_ref, gr_ref, xa_ref, dw_ref, gl_ref, dec_ref,
    out_ref, kb_ref, acc_ref, ge_ref,
):
    rows, main, _ = gconv_ref.shape
    high, wmain, chans = xa_ref.shape
    strip = main // SUBL
    wide = wmain // SUBL
    ln = slice(h * LANES, (h + 1) * LANES)
    for o in range(KSIZE * KSIZE):
        kb_ref[o] = jnp.broadcast_to(dw_ref[o : o + 1, ln].astype(F32), (SUBL, LANES))
    acc_ref[...] = jnp.zeros_like(acc_ref)
    ge_ref[...] = jnp.zeros_like(ge_ref)
    centre = gr_ref[:, ln].astype(F32).reshape(rows, main, LANES)
    ge_ref[RIM : RIM + rows, RIM * SUBL : RIM * SUBL + main, :] = centre

    def conv_back(y, c):
        g = gconv_ref[y, :, ln].reshape(strip, SUBL, LANES)
        for a in range(KSIZE):
            e = enc_ref[y + a, :, ln].reshape(wide, SUBL, LANES)
            out = [ge_ref[y + a, j * SUBL : (j + 1) * SUBL, :] for j in range(wide)]
            for b in range(KSIZE):
                o = a * KSIZE + b
                acc_ref[o] += jnp.sum(g * e[b : b + strip], axis=0)
                k = kb_ref[o]
                for j in range(strip):
                    out[j + b] = out[j + b] + g[j] * k
            for j in range(wide):
                ge_ref[y + a, j * SUBL : (j + 1) * SUBL, :] = out[j]
        return c

    lax.fori_loop(0, rows, conv_back, 0)
    xa = xa_ref[...].reshape(high * wmain, chans).astype(BF16)
    ge = ge_ref[...].reshape(high * wmain, LANES).astype(BF16)
    out_ref[...] = jnp.zeros_like(out_ref)
    out_ref[0:chans, :] = tn(xa, ge)
    out_ref[AT_DW : AT_DW + KSIZE * KSIZE, :] = jnp.sum(acc_ref[...], axis=1)
    out_ref[AT_GAIN : AT_GAIN + SUBL, :] = gl_ref[:, ln]
    out_ref[AT_DEC : AT_DEC + dec_ref.shape[0], :] = dec_ref[:, ln]


def vmem(n):
    return [pl.BlockSpec(memory_space=pltpu.VMEM) for _ in range(n)]


def grant(mib):
    return pltpu.CompilerParams(vmem_limit_bytes=mib << 20)


def swapped(value, axis, d):
    size = lax.axis_size(axis)
    return lax.ppermute(value, axis, [(i, i ^ d) for i in range(size)])


def pick_kernel(keep_ref, recv_ref, out_ref):
    out_ref[...] = (keep_ref[...] + recv_ref[...].astype(F32)).astype(out_ref.dtype)


def block_kernel(gate_ref, own_ref, *refs):
    base_ref, out_refs = refs[QUAD - 1], refs[QUAD:]
    total = own_ref[...]
    for ref in refs[: QUAD - 1]:
        total = total + ref[...].astype(F32)
    base_ref[...] = total[0]
    for g in range(1, len(out_refs) + 1):
        out_refs[g - 1][...] = total[g].astype(BF16)


def total_kernel(gate_ref, base_ref, *refs):
    total = base_ref[...]
    for ref in refs[:-1]:
        total = total + ref[...].astype(F32)
    refs[-1][...] = total.astype(BF16)


def hold_kernel(small_ref, *refs):
    out_ref = refs[-1]
    slots, tall, _ = out_ref.shape
    deep = refs[0].shape[1]
    for g in range(slots):
        out_ref[g, :, 0:deep] = refs[g][...]
    high = slots * tall
    for i in range(small_ref.shape[0] // high):
        at = deep + i * LANES
        block = small_ref[i * high : (i + 1) * high, :]
        out_ref[:, :, at : at + LANES] = block.reshape(slots, tall, LANES)


def halve_kernel(a_ref, b_ref, keep_ref, send_ref):
    first = lax.axis_index("sub") == 0
    a, b = a_ref[...], b_ref[...]
    keep_ref[...] = jnp.where(first, a, b)
    send_ref[...] = jnp.where(first, b, a).astype(BF16)


def pair_kernel(mine_ref, other_ref, out_ref):
    out_ref[...] = (mine_ref[...].astype(F32) + other_ref[...].astype(F32)).astype(BF16)


def spread_kernel(*refs):
    mine, other = refs[:QUAD], refs[QUAD : 2 * QUAD]
    up_ref, down_ref, enc_ref, dw_ref, gain_ref, dec_ref, loss_ref = refs[2 * QUAD : -2]
    small_ref, turned_ref = refs[-2:]
    slots, tall, _ = mine[0].shape
    width, hid = up_ref.shape
    chans = enc_ref.shape[0]
    band = lax.axis_index("band")
    sub = lax.axis_index("sub")
    high = slots * tall
    first = sub == 0
    for d in range(QUAD):
        for g in range(slots):
            rows = pl.ds(pl.multiple_of((band ^ reach(d, g)) * tall, tall), tall)
            one = mine[d][g, :, 0:hid].astype(F32)
            two = other[d][g, :, 0:hid].astype(F32)
            up_ref[rows, :] = jnp.where(first, one, two)
            turned_ref[rows, :] = jnp.where(first, two, one)
    for side, core in ((mine, sub), (other, 1 - sub)):
        lanes = pl.ds(pl.multiple_of(core * LANES, LANES), LANES)
        for i in range(SMALL_ROWS // high):
            ln = slice(hid + i * LANES, hid + (i + 1) * LANES)
            a, b, c, e = [side[d][:, :, ln].astype(F32) for d in range(QUAD)]
            small_ref[i * high : (i + 1) * high, lanes] = ((a + b) + (c + e)).reshape(high, LANES)
    for q in range(hid // width):
        ln = slice(q * width, (q + 1) * width)
        down_ref[ln, :] = turned_ref[:, ln].T
    enc_ref[...] = small_ref[0:chans, :]
    dec_ref[...] = small_ref[AT_DEC : AT_DEC + chans, :]
    dw_ref[...] = small_ref[AT_DW : AT_DW + KSIZE * KSIZE, :]
    gain_ref[...] = small_ref[AT_GAIN : AT_GAIN + 1, :]
    loss_ref[...] = jnp.sum(small_ref[AT_LOSS : AT_LOSS + 3, :], axis=(0, 1), keepdims=True)


def local(body, out_shape, mib, name, *args, gates=(), scratch=(), cost=None):
    many = isinstance(out_shape, (list, tuple))
    return pl.pallas_call(
        body,
        out_shape=out_shape,
        in_specs=[pl.BlockSpec(memory_space=pl.ANY) for _ in gates] + vmem(len(args)),
        out_specs=vmem(len(out_shape)) if many else vmem(1)[0],
        scratch_shapes=list(scratch), name=name, compiler_params=grant(mib), cost_estimate=cost,
    )(*gates, *args)


def summed(keep, send, inner, shapes):
    enc, gconv, gr, xa, dw_kernel, gl, dec = inner
    blocks, tall, deep = keep[0].shape
    n = lax.axis_size("band")
    piece = (tall, deep)
    slab = (blocks,) + piece
    high, wmain, _ = xa.shape

    def back(h, gate):
        return local(
            lambda *r: back_kernel(h, *r),
            jax.ShapeDtypeStruct((SMALL_ROWS, LANES), F32), 10, f"back{h}",
            enc, gconv, gr, xa, dw_kernel, gl, dec,
            gates=(gate,),
            scratch=[
                pltpu.VMEM((KSIZE * KSIZE, SUBL, LANES), F32),
                pltpu.VMEM((KSIZE * KSIZE, SUBL, LANES), F32),
                pltpu.VMEM((high, wmain, LANES), F32),
            ],
            cost=pl.CostEstimate(flops=3_000_000_000, bytes_accessed=18_000_000, transcendentals=0),
        )

    got = []
    for d in range(QUAD - 1, -1, -1):
        shape = jax.ShapeDtypeStruct(slab, BF16 if d else F32)
        part = local(pick_kernel, shape, 6, f"pick{d}", keep[d], swapped(send[d], "sub", 1))
        got.append(swapped(part, "band", d) if d else part)
    small_a = back(0, got[-1])
    base, *far = local(
        block_kernel,
        [jax.ShapeDtypeStruct(piece, F32)] + [jax.ShapeDtypeStruct(piece, BF16)] * (blocks - 1),
        8, "block", got[-1], *got[:-1], gates=(small_a,),
    )
    got = [swapped(far[g - 1], "band", QUAD * g) for g in range(1, blocks)]
    small_b = back(1, far[0])
    total = local(
        total_kernel, jax.ShapeDtypeStruct(piece, BF16), 4, "total", base, *got, gates=(small_b,)
    )
    half = (SMALL_ROWS, LANES)
    s_keep, s_send = local(
        halve_kernel,
        [jax.ShapeDtypeStruct(half, F32), jax.ShapeDtypeStruct(half, BF16)],
        4, "halve", small_a, small_b,
    )
    small = local(
        pick_kernel, jax.ShapeDtypeStruct(half, BF16), 4, "chip", s_keep, swapped(s_send, "sub", 1)
    )
    got = [swapped(total, "band", QUAD * g) for g in range(1, blocks)]
    step = QUAD
    while step < n:
        small = local(
            pair_kernel, jax.ShapeDtypeStruct(half, BF16), 4, "pair",
            small, swapped(small, "band", step),
        )
        step *= 2
    hold = local(
        hold_kernel,
        jax.ShapeDtypeStruct((blocks, tall, deep + SMALL_ROWS // (blocks * tall) * LANES), BF16),
        4, "hold", small, total, *got,
    )
    mine = [hold] + [swapped(hold, "band", d) for d in range(QUAD - 1, 0, -1)][::-1]
    other = [swapped(value, "sub", 1) for value in mine]
    width, hid = shapes[0]
    return local(
        spread_kernel, [jax.ShapeDtypeStruct(s, F32) for s in shapes], 16, "spread",
        *mine, *other,
        scratch=[
            pltpu.VMEM((SMALL_ROWS, width), F32),
            pltpu.VMEM((width, hid), F32),
        ],
    )


def shards(state, target, tile_plan, w_enc, dw_kernel, norm_gain, w_up, w_down, w_dec):
    chans, rows, cols = state.shape
    width = w_enc.shape[1]
    hid = w_up.shape[1]
    main = cols
    wmain = cols + 2 * RIM * SUBL
    high = rows + 2 * RIM
    n_band = lax.axis_size("band")

    st = state.transpose(1, 0, 2)
    tgt = target.transpose(1, 0, 2)
    edges = jnp.concatenate([st[:, :, cols - RIM :], st[:, :, :RIM]], axis=2)
    other = swapped(edges, "sub", 1)
    last = jnp.concatenate([st[rows - RIM :], other[rows - RIM :]], axis=2)
    first = jnp.concatenate([st[:RIM], other[:RIM]], axis=2)
    odd = (lax.axis_index("band") & 1) == 1
    near = lax.ppermute(
        jnp.where(odd, first, last), "band", [(i, i ^ 1) for i in range(n_band)]
    )
    pairs = [(i, i + 1) for i in range(1, n_band - 1, 2)]
    to_far = jnp.where(odd, last, first)
    far = lax.ppermute(to_far, "band", pairs + [(j, i) for i, j in pairs])

    cells = rows * main
    chunk = GROUP * main
    n = n_band
    tall = width // n
    slab = (n // QUAD, tall, hid)
    enc, xa, nrm, kb = local(
        early_kernel,
        [
            jax.ShapeDtypeStruct((high, wmain, width), F32),
            jax.ShapeDtypeStruct((high, wmain, chans), F32),
            jax.ShapeDtypeStruct((rows, main, width), F32),
            jax.ShapeDtypeStruct((KSIZE * KSIZE, SUBL, width), F32),
        ],
        12, "early", st, other, w_enc, dw_kernel, gates=(to_far,),
        cost=pl.CostEstimate(flops=3_000_000_000, bytes_accessed=15_000_000, transcendentals=0),
    )
    new, *rest = pl.pallas_call(
        step_kernel,
        out_shape=[
            jax.ShapeDtypeStruct((rows, chans, cols), BF16),
            *[jax.ShapeDtypeStruct(slab, F32)] * QUAD,
            *[jax.ShapeDtypeStruct(slab, BF16)] * QUAD,
            jax.ShapeDtypeStruct((high, wmain, width), F32),
            jax.ShapeDtypeStruct((rows, main, width), F32),
            jax.ShapeDtypeStruct((cells, width), BF16),
            jax.ShapeDtypeStruct((high, wmain, chans), F32),
            jax.ShapeDtypeStruct((SUBL, width), F32),
            jax.ShapeDtypeStruct((AT_DW - AT_DEC, width), F32),
        ],
        in_specs=vmem(14), out_specs=vmem(7 + 2 * QUAD),
        scratch_shapes=[
            pltpu.VMEM((chunk, LANES), F32),
            pltpu.VMEM((cells, hid), BF16),
            pltpu.VMEM((chunk, hid), F32),
            pltpu.VMEM((cells, hid), BF16),
            pltpu.VMEM((chunk, width), F32),
            pltpu.VMEM((cells, width), BF16),
            pltpu.VMEM((chunk, width), F32),
            pltpu.VMEM((n, tall, 2 * hid), F32),
        ],
        name="step",
        compiler_params=grant(36),
    )(
        tile_plan, st, near, far, enc, xa, nrm, kb, tgt,
        w_enc, norm_gain.reshape(1, width), w_up, w_down, w_dec.T,
    )
    g_up, g_down, g_enc, g_dw, g_gain, g_dec, loss = summed(
        rest[:QUAD], rest[QUAD : 2 * QUAD],
        (*rest[2 * QUAD : 2 * QUAD + 4], dw_kernel, *rest[2 * QUAD + 4 :]),
        [(width, hid), (hid, width), (chans, width), dw_kernel.shape, (1, width), (chans, width), (1, 1)],
    )
    return (
        new.transpose(1, 0, 2), loss.reshape(1), g_enc, g_dw, g_gain.reshape(width),
        g_up, g_down, g_dec.T,
    )


def solution(mesh):
    return jax.shard_map(
        shards,
        mesh=mesh,
        in_specs=(
            P("groups", "band", "sub"),
            P("groups", "band", "sub"),
            P("groups", None),
            P(),
            P(),
            P(),
            P(),
            P(),
            P(),
        ),
        out_specs=(
            P("groups", "band", "sub"),
            P("groups"),
            P("groups", None),
            P("groups", None),
            P("groups"),
            P("groups", None),
            P("groups", None),
            P("groups", None),
        ),
        check_vma=False,
    )
```
